128 devices in a mesh: slab: 8 (over z, core), tile: 16 (over y, x).
Axes of the slice: x: 4, y: 4, z: 4, core: 2. Of those that a mesh axis runs over, the one named last changes fastest.
Arguments:
- owner: int32 [32768, 1], P(('slab', 'tile')), may hold values from 0 to 127; in each aligned block of 256 rows (0 to 255, 256 to 511, ...) at most 4 rows name the same one
- block_base: int32 [3, 32768], P(None, ('slab', 'tile')), may hold values from 0 to 124, as said below
- spline_weights: float32 [12, 32768], P(None, ('slab', 'tile')), may hold values from 0.25 to 1
- measured: float32 [3, 32768], P(None, ('slab', 'tile')), may hold values from -6 to 6
- div_weight: float32 [1], replicated, may hold values from 0.05 to 0.5
- bend_weight: float32 [1], replicated, may hold values from 0.002 to 0.02
Outputs:
- solution: float32 [3, 32, 128, 128], P(None, 'slab', 'tile')
- residual: float32 [3, 32, 128, 128], P(None, 'slab', 'tile')
The draws below stay inside these ranges and needn't reach their ends.
Inputs may be any that keep to these rules, and one draw needn't show every extreme that they name: `block_base`: row 0 is below 4, row 1 below 8, row 2 at most 124; each row reaches its largest value and 0. Among the 256 samples of one device at most 4 name the same owner.
All inputs are finite; a program needn't handle non-finite values.
Results may differ from the reference program's by a relative error of at most 0.0003.
Values sent between devices are 32-bit elements; how exact they have to be, the bound alone decides.
A program may use at most 64 MiB of HBM per device.

```python
import math
import jax
import jax.numpy as jnp
import numpy as np
from jax import lax

CZ = 4
CX = 8
NY = 128
S_DEV = 256
ITERS = 2
CAP = 4
NZ = 32
NX = 128
SAMPLES = 32768
N_TILE = 16
DEVICES = 128


def draw_block_base(key, part):
    upper = jnp.array([CZ, CX, NY - 3], jnp.int32)[:, None]
    values = jax.random.randint(key, (3, SAMPLES), 0, upper)
    values = values.at[:, 0].set(upper[:, 0] - 1)
    values = values.at[:, 1].set(0)
    return values.astype(jnp.int32)


def block_scale(own_key, dims, shards, low, high):
    level = 1.0
    for dim, parts in shards:
        heights = jax.random.uniform(jax.random.fold_in(jax.random.fold_in(own_key, 6), dim), (parts,), jnp.float32, low / len(shards), high / len(shards))
        level = level * jnp.repeat(jnp.exp(heights), dims[dim] // parts).reshape((-1,) + (1,) * (len(dims) - 1 - dim))
    return level


def deal_out(rng, own, number, rows, amount, top, bound, lean):
    order = jax.random.permutation(rng, amount)
    packed, usual = portions_of(amount, rows * top, bound, lean, True), portions_of(amount, rows * top, bound, lean, False)
    places = jnp.arange(amount)

    def named(tallies, turn):
        used = int((tallies > 0).sum())
        fixed = max(1, used // 4)
        moved = fixed + (places - fixed + turn * (used - fixed)) % max(1, amount - fixed)
        return jnp.zeros((amount,), jnp.int32).at[order[jnp.where(places < fixed, places, moved)]].set(jnp.asarray(tallies, jnp.int32))

    tallies = jnp.where(number % 4 == 0, named(packed, number // 4), named(usual, number - number // 4 - 1))
    mixed = jax.random.permutation(jax.random.fold_in(own, 3), amount)
    giver, sink = mixed[0:amount // 2 * 2:2], mixed[1:amount // 2 * 2:2]
    slack = jnp.minimum(tallies[giver] - 1, bound - tallies[sink]) // 2
    slack = jnp.where((giver == order[0]) | (sink == order[0]) | (tallies[sink] == 0), 0, jnp.maximum(slack, 0))
    moved = jax.random.randint(jax.random.fold_in(own, 4), (amount // 2,), 0, 1 << 20) % (slack + 1)
    tallies = tallies.at[giver].add(-moved).at[sink].add(moved)
    items = jnp.searchsorted(jnp.cumsum(tallies), jnp.arange(rows * top), side="right").astype(jnp.int32)
    table = items.reshape(top, rows).T
    table = table[jax.random.permutation(jax.random.fold_in(own, 1), rows)]
    turn = jax.random.randint(jax.random.fold_in(own, 2), (rows, 1), 0, top)
    return jnp.take_along_axis(table, (jnp.arange(top)[None, :] + turn) % top, axis=1)


def portions_of(count, total, reach, lean, full):
    weights = [(1 << 20) // math.isqrt(grade ** lean) + 1 for grade in range(1, count + 1)]
    largest = reach if full else min(reach, max(-(-total // count), total * weights[0] // sum(weights)))
    least = 1 if total - largest >= count - 1 else 0
    given, spare = [largest] + [least] * (count - 1), total - largest - least * (count - 1)
    while spare > 0:
        movable = [i for i in range(1, count) if given[i] < largest] or [i for i in range(1, count) if given[i] < reach]
        whole, left = sum([weights[i] for i in movable]), spare
        for i in movable:
            addition = min(reach - given[i], max(1, left * weights[i] // whole), spare)
            given[i] = given[i] + addition
            spare = spare - addition
    return np.array(given)


def bell_draw(own_key, shape, scale, limit, split=(), kind=jnp.bfloat16):
    values = scale * jax.random.normal(own_key, shape, jnp.float32)
    if split:
        values = values * block_scale(own_key, shape, split, -0.22, 0.18)
    return jnp.clip(values, -limit, limit).astype(kind)


def setup_inputs(seed: int = 0) -> dict:
    seeds = jax.random.split(jax.random.key(seed), 7)
    owner_keys = jax.random.split(jax.random.fold_in(seeds[0], 1), SAMPLES // S_DEV)
    owner_turns = jax.random.permutation(jax.random.fold_in(seeds[0], 3), SAMPLES // S_DEV)
    owner = jax.vmap(lambda own, number: deal_out(jax.random.fold_in(seeds[0], 2), own, number, S_DEV, DEVICES, 1, CAP, 2))(owner_keys, owner_turns).reshape((SAMPLES, 1))
    block_base = draw_block_base(jax.random.fold_in(seeds[6], 71), 0)
    spline_weights = jnp.clip(0.25 + 0.75 * jax.random.uniform(seeds[2], (12, SAMPLES), jnp.float32) ** block_scale(seeds[2], (12, SAMPLES), ((1, 128),), -0.2, 0.2), 0.25, 1.0)
    measured = bell_draw(seeds[3], (3, SAMPLES), 1.0, 6.0, ((1, 128),), jnp.float32)
    div_weight = jnp.clip(jnp.exp(jax.random.uniform(seeds[4], (1,), jnp.float32, math.log(0.05), math.log(0.5))), 0.05, 0.5)
    bend_weight = jnp.clip(jnp.exp(jax.random.uniform(seeds[5], (1,), jnp.float32, math.log(0.002), math.log(0.02))), 0.002, 0.02)
    return dict(owner=owner, block_base=block_base, spline_weights=spline_weights, measured=measured, div_weight=div_weight, bend_weight=bend_weight)


def neighbours(field):
    middle = field[:, 1:-1, 1:-1, :]
    total = field[:, 2:, 1:-1, :] + field[:, :-2, 1:-1, :] + field[:, 1:-1, 2:, :] + field[:, 1:-1, :-2, :]
    padded = jnp.pad(middle, ((0, 0), (0, 0), (0, 0), (1, 1)))
    total = total + padded[..., 2:] + padded[..., :-2]
    return total - 6.0 * middle


def divergence(field):
    along_z = field[0, 2:, 1:-1, :] - field[0, 1:-1, 1:-1, :]
    along_x = field[1, 1:-1, 2:, :] - field[1, 1:-1, 1:-1, :]
    centre = field[2, 1:-1, 1:-1, :]
    along_y = jnp.pad(centre[..., 1:], ((0, 0), (0, 0), (0, 1))) - centre
    return along_z + along_x + along_y


def divergence_adjoint(values):
    centre = values[1:-1, 1:-1, :]
    first = values[:-2, 1:-1, :] - centre
    second = values[1:-1, :-2, :] - centre
    third = jnp.pad(centre[..., :-1], ((0, 0), (0, 0), (1, 0))) - centre
    return jnp.stack([first, second, third])


def spline_tables(owned, base, weights):
    offsets = jnp.arange(64, dtype=jnp.int32)
    off_z = offsets // 16
    off_x = (offsets // 4) % 4
    off_y = offsets % 4
    z_start = (owned // N_TILE) * CZ + base[0]
    x_start = (owned % N_TILE) * CX + base[1]
    index = ((z_start[None] + off_z[:, None]) * (NX + 3) + x_start[None] + off_x[:, None]) * NY + base[2][None] + off_y[:, None]
    factor = (weights[0:4][:, None, None, :] * weights[4:8][None, :, None, :] * weights[8:12][None, None, :, :]).reshape(64, -1)
    return index.astype(jnp.int32), factor


def scatter_blocks(blocks, values_of):
    def step(total, item):
        owned, base, weights, extra = item
        index, factor = spline_tables(owned, base, weights)
        values = values_of(index, factor, extra)
        return total.at[:, index].add(values[:, None, :] * factor[None]), None
    zeros = jnp.zeros((3, (NZ + 3) * (NX + 3) * NY), jnp.float32)
    total, _ = lax.scan(step, zeros, blocks)
    return total.reshape(3, NZ + 3, NX + 3, NY)[:, :NZ, :NX, :]


def reference(owner, block_base, spline_weights, measured, div_weight, bend_weight):
    blocks = (owner[:, 0].reshape(-1, S_DEV),
              block_base.reshape(3, -1, S_DEV).transpose(1, 0, 2),
              spline_weights.reshape(12, -1, S_DEV).transpose(1, 0, 2),
              measured.reshape(3, -1, S_DEV).transpose(1, 0, 2))
    right_side = scatter_blocks(blocks, lambda index, factor, extra: extra)

    def operate(field):
        padded = jnp.pad(field, ((0, 0), (0, 3), (0, 3), (0, 0))).reshape(3, -1)

        def read_values(index, factor, extra):
            return jnp.sum(padded[:, index] * factor[None], axis=1)
        image = scatter_blocks(blocks, read_values)
        cycle = jnp.pad(field, ((0, 0), (1, 1), (1, 1), (0, 0)))
        smooth = neighbours(cycle)
        source = divergence(cycle)
        bent = neighbours(jnp.pad(smooth, ((0, 0), (1, 1), (1, 1), (0, 0))))
        pushed = divergence_adjoint(jnp.pad(source, ((1, 1), (1, 1), (0, 0))))
        return image + div_weight[0] * pushed + bend_weight[0] * bent

    solution = jnp.zeros_like(right_side)
    residual = right_side
    direction = right_side
    norm_now = jnp.sum(residual * residual)
    for step in range(ITERS):
        image = operate(direction)
        alpha = norm_now / jnp.sum(direction * image)
        solution = solution + alpha * direction
        residual = residual - alpha * image
        norm_next = jnp.sum(residual * residual)
        direction = residual + (norm_next / norm_now) * direction
        norm_now = norm_next
    return solution, residual
```

```python
import functools

import jax
import jax.numpy as jnp
from jax import lax
from jax.experimental import pallas as pl
from jax.experimental.pallas import tpu as pltpu
from jax.sharding import PartitionSpec as P

CZ = 4
CX = 8
NY = 128
CAP = 4
LANES = 128
F32 = jnp.float32
BF16 = jnp.bfloat16
NT = (((1,), (1,)), ((), ()))
NN = (((1,), (0,)), ((), ()))
HALO = (
    ((-1, -1), (0, 3), (0, 3), 4, 8),
    ((0, -1), (0, 4), (0, 3), 0, 8),
    ((0, 1), (0, 4), (6, 2), 0, 14),
    ((-1, 0), (0, 3), (0, 8), 4, 0),
    ((1, 0), (2, 2), (0, 8), 7, 0),
    ((1, 1), (3, 1), (7, 1), 8, 15),
    ((1, -1), (3, 1), (0, 1), 8, 8),
    ((-1, 1), (0, 1), (7, 1), 4, 15),
)
SPILL = (
    ((1, 1), (4, 3), (8, 3)),
    ((0, 1), (0, 4), (8, 3)),
    ((1, 0), (4, 3), (0, 8)),
)


def split(value):
    high = value.astype(BF16)
    return high, (value - high.astype(F32)).astype(BF16)


def product(left, right, dims):
    dot = functools.partial(lax.dot_general, dimension_numbers=dims, preferred_element_type=F32)
    return dot(left[0], right[0]) + (dot(left[0], right[1]) + dot(left[1], right[0]))


def kernel(
    slabs, tiles, owner_ref, base_ref, spline_ref, measured_ref, div_ref, bend_ref,
    solution_ref, residual_ref,
    pay, out_rows, by_slab, turned, by_tile,
    partial, spill, field, bent, source, sum_slab, sum_tile,
    pass_send, pass_slab_recv, pass_tile_recv, spill_send, spill_recv, halo_send, halo_recv,
    sum_send, sum_slab_recv, sum_tile_recv,
):
    devices = slabs * tiles
    slab, tile = lax.axis_index("slab"), lax.axis_index("tile")
    count = owner_ref.shape[1]

    barrier = pltpu.get_barrier_semaphore()

    def mesh_at(s, t):
        return {"slab": s, "tile": t}

    def other_slab(step):
        return lax.rem(slab + step, slabs)

    def other_tile(step):
        return lax.rem(tile + step, tiles)

    field[...] = jnp.zeros_like(field)
    spill[...] = jnp.zeros_like(spill)

    for step in range(1, slabs):
        pl.semaphore_signal(barrier, inc=1, device_id=mesh_at(other_slab(step), tile))
    for step in range(1, tiles):
        pl.semaphore_signal(barrier, inc=1, device_id=mesh_at(slab, other_tile(step)))
    for s in (1, slabs - 1):
        for t in (1, tiles - 1):
            pl.semaphore_signal(barrier, inc=1, device_id=mesh_at(other_slab(s), other_tile(t)))

    pay[...] = jnp.zeros_like(pay)
    pay[0:12, :] = spline_ref[...]
    pay[12:15, :] = measured_ref[...]
    pay[15:18, :] = base_ref[...].astype(F32)
    owner = owner_ref[...]
    onehot = (lax.broadcasted_iota(jnp.int32, (devices, count), 0) == owner).astype(F32)
    onehot_b = onehot.astype(BF16)
    earlier = (
        lax.broadcasted_iota(jnp.int32, (count, count), 0)
        < lax.broadcasted_iota(jnp.int32, (count, count), 1)
    ).astype(BF16)
    before = lax.dot_general(onehot_b, earlier, NN, preferred_element_type=F32)
    rank = jnp.sum(onehot * before, axis=0, keepdims=True)
    payload = pay[...]
    slots = jnp.concatenate([jnp.where(rank == k, payload, 0.0) for k in range(CAP)], axis=0)
    high, low = split(slots)
    lowest = (slots - high.astype(F32) - low.astype(F32)).astype(BF16)
    rows = [lax.dot_general(onehot_b, part, NT, preferred_element_type=F32) for part in (high, low, lowest)]
    out_rows[...] = ((rows[0] + rows[1]) + rows[2]).reshape(slabs, tiles, LANES)

    pl.semaphore_wait(barrier, slabs - 1 + tiles - 1 + 4)

    sends = []
    for step in range(1, slabs):
        to = other_slab(step)
        copy = pltpu.make_async_remote_copy(
            src_ref=out_rows.at[to], dst_ref=by_slab.at[slab],
            send_sem=pass_send.at[step], recv_sem=pass_slab_recv.at[slab],
            device_id=mesh_at(to, tile),
        )
        copy.start()
        sends.append(copy)
    by_slab[slab] = out_rows[slab]
    for step in range(1, slabs):
        origin = other_slab(step)
        pltpu.make_async_remote_copy(
            src_ref=out_rows.at[origin], dst_ref=by_slab.at[origin],
            send_sem=pass_send.at[step], recv_sem=pass_slab_recv.at[origin],
            device_id=mesh_at(origin, tile),
        ).wait_recv()
    for s in range(slabs):
        turned[pl.ds(s, tiles, stride=slabs), :] = by_slab[s]
    for step in range(1, tiles):
        to = other_tile(step)
        copy = pltpu.make_async_remote_copy(
            src_ref=turned.at[pl.ds(to * slabs, slabs)], dst_ref=by_tile.at[pl.ds(tile * slabs, slabs)],
            send_sem=pass_send.at[slabs + step], recv_sem=pass_tile_recv.at[tile],
            device_id=mesh_at(slab, to),
        )
        copy.start()
        sends.append(copy)
    by_tile[pl.ds(tile * slabs, slabs), :] = turned[pl.ds(tile * slabs, slabs), :]
    for step in range(1, tiles):
        origin = other_tile(step)
        pltpu.make_async_remote_copy(
            src_ref=turned.at[pl.ds(origin * slabs, slabs)], dst_ref=by_tile.at[pl.ds(origin * slabs, slabs)],
            send_sem=pass_send.at[slabs + step], recv_sem=pass_tile_recv.at[origin],
            device_id=mesh_at(slab, origin),
        ).wait_recv()

    lanes_first = by_tile[...].T
    owned = jnp.concatenate([lanes_first[32 * k : 32 * k + 32] for k in range(CAP)], axis=1)
    total = owned.shape[1]

    def spread_weights(cells, base, first):
        offset = lax.broadcasted_iota(jnp.int32, (cells, total), 0).astype(F32) - owned[base : base + 1]
        result = jnp.zeros((cells, total), F32)
        for step in range(4):
            result = jnp.where(offset == float(step), owned[first + step : first + step + 1], result)
        return result

    weight_z = spread_weights(8, 15, 0)
    weight_x = spread_weights(16, 16, 4)
    weight_y = spread_weights(NY, 17, 8)
    plane = jnp.concatenate([weight_z[z : z + 1] * weight_x for z in range(CZ + 3)], axis=0)
    plane_parts = split(plane)

    def send_spread(turn, values):
        sends = []
        columns = split(jnp.concatenate([weight_y * values[c] for c in range(3)], axis=0))
        partial[turn] = product(plane_parts, columns, NT).reshape(CZ + 3, 16, 3 * NY)
        for number, ((s, t), z, x) in enumerate(SPILL):
            copy = spill_copy(turn, number)

            @pl.when(exists(s, t))
            def _():
                copy.start()

    def exists(s, t):
        inside = None
        if s:
            inside = (slab < slabs - 1) if s > 0 else (slab > 0)
        if t:
            along = (tile < tiles - 1) if t > 0 else (tile > 0)
            inside = along if inside is None else jnp.logical_and(inside, along)
        return inside

    def toward(s, t):
        return mesh_at(lax.rem(slab + s + slabs, slabs), lax.rem(tile + t + tiles, tiles))

    def spill_copy(turn, number):
        (s, t), (z, zs), (x, xs) = SPILL[number]
        return pltpu.make_async_remote_copy(
            src_ref=partial.at[turn, pl.ds(z, zs), pl.ds(x, xs)],
            dst_ref=spill.at[turn, number, pl.ds(0, zs), pl.ds(0, xs)],
            send_sem=spill_send.at[turn, number], recv_sem=spill_recv.at[turn, number],
            device_id=toward(s, t),
        )

    def gather_spread(turn):
        for number, ((s, t), z, x) in enumerate(SPILL):

            @pl.when(exists(-s, -t))
            def _():
                spill_copy(turn, number).wait_recv()

        result = []
        for z in range(CZ):
            value = partial[turn, z, 0:CX] + spill[turn, 1, z]
            if z < 3:
                value = value + (spill[turn, 0, z] + spill[turn, 2, z])
            result.append(value)
        return result

    def halo_copy(turn, number):
        (s, t), (z, zs), (x, xs), to_z, to_x = HALO[number]
        return pltpu.make_async_remote_copy(
            src_ref=field.at[turn, pl.ds(z, zs), pl.ds(x, xs)],
            dst_ref=field.at[turn, pl.ds(to_z, zs), pl.ds(to_x, xs)],
            send_sem=halo_send.at[turn, number], recv_sem=halo_recv.at[turn, number],
            device_id=toward(s, t),
        )

    def send_halo(turn):
        for number, entry in enumerate(HALO):
            copy = halo_copy(turn, number)

            @pl.when(exists(*entry[0]))
            def _():
                copy.start()

    def wait_halo(turn):
        for number, entry in enumerate(HALO):

            @pl.when(exists(-entry[0][0], -entry[0][1]))
            def _():
                halo_copy(turn, number).wait_recv()

    def read_samples(turn):
        readings = []
        for c in range(3):
            part = field[turn, 0 : CZ + 3, :, c * NY : (c + 1) * NY].reshape((CZ + 3) * 16, NY).T
            seen = product(split(part), plane_parts, NN)
            readings.append(jnp.sum(seen * weight_y, axis=0, keepdims=True))
        return readings

    lane = lax.broadcasted_iota(jnp.int32, (16, NY), 1)
    place = lax.broadcasted_iota(jnp.int32, (16, NY), 0)
    has_low_z, has_high_z = slab > 0, slab < slabs - 1
    inside_x = (place < CX) | ((place == CX) & (tile < tiles - 1)) | ((place == 15) & (tile > 0))

    def after_y(value):
        return jnp.where(lane == NY - 1, 0.0, pltpu.roll(value, NY - 1, 1))

    def before_y(value):
        return jnp.where(lane == 0, 0.0, pltpu.roll(value, 1, 1))

    def after_x(value):
        return pltpu.roll(value, 15, 0)

    def before_x(value):
        return pltpu.roll(value, 1, 0)

    def around(below, middle, above):
        total = (above + below) + (after_x(middle) + before_x(middle))
        return total + (after_y(middle) + before_y(middle)) - 6.0 * middle

    def cell(turn, c, z):
        return field[turn, z if z >= 0 else z + 9, :, c * NY : (c + 1) * NY]

    def inside(value, z):
        keep = inside_x
        if z < 0:
            keep = keep & has_low_z
        if z >= CZ:
            keep = keep & has_high_z
        return jnp.where(keep, value, 0.0)

    def smooth(turn):
        for c in range(3):
            for z in range(-1, CZ + 1):
                value = around(cell(turn, c, z - 1), cell(turn, c, z), cell(turn, c, z + 1))
                bent[turn, c, z + 1] = inside(value, z)
        for z in range(-1, CZ):
            along_z = cell(turn, 0, z + 1) - cell(turn, 0, z)
            along_x = after_x(cell(turn, 1, z)) - cell(turn, 1, z)
            along_y = after_y(cell(turn, 2, z)) - cell(turn, 2, z)
            source[turn, z + 1] = inside(along_z + along_x + along_y, z)

    div_weight = div_ref[0]
    bend_weight = bend_ref[0]

    def penalties(turn, c, z):
        here = source[turn, z + 1]
        if c == 0:
            pushed = source[turn, z] - here
        elif c == 1:
            pushed = before_x(here) - here
        else:
            pushed = before_y(here) - here
        again = around(bent[turn, c, z], bent[turn, c, z + 1], bent[turn, c, z + 2])
        return (div_weight * pushed + bend_weight * again)[0:CX]

    def all_penalties(turn):
        return [
            jnp.concatenate([penalties(turn, c, z) for c in range(3)], axis=1) for z in range(CZ)
        ]

    def one(value):
        return jnp.sum(jnp.sum(value, axis=0, keepdims=True), axis=1, keepdims=True)

    row_lane = lax.broadcasted_iota(jnp.int32, (1, LANES), 1)

    def sum_copy(turn, stage, step, incoming):
        buffer, size, mine, peer = (
            (sum_slab, slabs, slab, other_slab(step)) if stage == 0 else (sum_tile, tiles, tile, other_tile(step))
        )
        received = sum_slab_recv if stage == 0 else sum_tile_recv
        where = peer if incoming else mine
        return pltpu.make_async_remote_copy(
            src_ref=buffer.at[turn, pl.ds(mine, 1)], dst_ref=buffer.at[turn, pl.ds(where, 1)],
            send_sem=sum_send.at[turn, stage, step], recv_sem=received.at[turn, where],
            device_id=mesh_at(peer, tile) if stage == 0 else mesh_at(slab, peer),
        )

    def start_sum(turn, values):
        row = jnp.zeros((1, LANES), F32)
        for number, value in enumerate(values):
            row = jnp.where(row_lane == number, value, row)
        sum_slab[turn, pl.ds(slab, 1)] = row
        for step in range(1, slabs):
            sum_copy(turn, 0, step, False).start()

    def turn_sum(turn):
        for step in range(1, slabs):
            sum_copy(turn, 0, step, True).wait_recv()
        sum_tile[turn, pl.ds(tile, 1)] = jnp.sum(sum_slab[turn], axis=0, keepdims=True)
        for step in range(1, tiles):
            sum_copy(turn, 1, step, False).start()

    def end_sum(turn, number):
        for step in range(1, tiles):
            sum_copy(turn, 1, step, True).wait_recv()
        row = jnp.sum(sum_tile[turn], axis=0, keepdims=True)
        return [row[:, i : i + 1] for i in range(number)]

    send_spread(0, [owned[12 + c : 13 + c] for c in range(3)])
    start = gather_spread(0)
    for z in range(CZ):
        field[0, z, 0:CX] = start[z]
    send_halo(0)
    square = one(functools.reduce(jnp.add, [v * v for v in start]))

    wait_halo(0)
    read_start = read_samples(0)
    send_spread(1, read_start)
    smooth(0)

    def energy(readings, sources, bends):
        seen = one(functools.reduce(jnp.add, [v * v for v in readings]))
        pushed = one(functools.reduce(jnp.add, [v * v for v in sources]))
        again = one(functools.reduce(jnp.add, [v * v for v in bends]))
        return seen + div_weight * pushed + bend_weight * again

    def own_source(turn):
        return [source[turn, z + 1, 0:CX] for z in range(CZ)]

    def own_bent(turn):
        return [bent[turn, c, z + 1, 0:CX] for c in range(3) for z in range(CZ)]

    start_sum(0, [square, energy(read_start, own_source(0), own_bent(0))])
    held = all_penalties(0)
    turn_sum(0)
    image = [v + p for v, p in zip(gather_spread(1), held)]
    for z in range(CZ):
        field[1, z, 0:CX] = image[z]
    send_halo(1)
    norm, curvature = end_sum(0, 2)
    step_size = norm / curvature
    left = [b - step_size * y for b, y in zip(start, image)]
    left_square = one(functools.reduce(jnp.add, [v * v for v in left]))
    left_image = one(functools.reduce(jnp.add, [v * y for v, y in zip(left, image)]))

    wait_halo(1)
    read_image = read_samples(1)
    smooth(1)
    left_energy = energy(
        [a - step_size * b for a, b in zip(read_start, read_image)],
        [a - step_size * b for a, b in zip(own_source(0), own_source(1))],
        [a - step_size * b for a, b in zip(own_bent(0), own_bent(1))],
    )
    start_sum(1, [left_square, left_image, left_energy])
    send_spread(2, read_image)
    held = all_penalties(1)
    turn_sum(1)
    second = [v + p for v, p in zip(gather_spread(2), held)]
    left_square, left_image, left_energy = end_sum(1, 3)

    ratio = left_square / norm
    bowed = left_energy + 2.0 * ratio * left_image + ratio * ratio * curvature
    step_next = left_square / bowed
    for z in range(CZ):
        direction = left[z] + ratio * start[z]
        pushed = (image[z] - step_size * second[z]) + ratio * image[z]
        answer = step_size * start[z] + step_next * direction
        rest = left[z] - step_next * pushed
        for c in range(3):
            solution_ref[c, z] = answer[:, c * NY : (c + 1) * NY]
            residual_ref[c, z] = rest[:, c * NY : (c + 1) * NY]

    for copy in sends:
        copy.wait_send()
    for turn in range(3):
        for number, ((s, t), z, x) in enumerate(SPILL):

            @pl.when(exists(s, t))
            def _():
                spill_copy(turn, number).wait_send()

    for turn in range(2):
        for number, entry in enumerate(HALO):

            @pl.when(exists(*entry[0]))
            def _():
                halo_copy(turn, number).wait_send()

        for step in range(1, slabs):
            sum_copy(turn, 0, step, False).wait_send()
        for step in range(1, tiles):
            sum_copy(turn, 1, step, False).wait_send()


def local(slabs, tiles, owner, block_base, spline_weights, measured, div_weight, bend_weight):
    devices = slabs * tiles
    count = owner.shape[0]
    vmem = pl.BlockSpec(memory_space=pltpu.VMEM)
    smem = pl.BlockSpec(memory_space=pltpu.SMEM)
    dma = pltpu.SemaphoreType.DMA
    wide = 3 * NY
    out = jax.ShapeDtypeStruct((3, CZ, CX, NY), F32)
    return pl.pallas_call(
        functools.partial(kernel, slabs, tiles),
        out_shape=(out, out),
        in_specs=[vmem] * 4 + [smem] * 2,
        out_specs=(vmem, vmem),
        scratch_shapes=[
            pltpu.VMEM((32, count), F32),
            pltpu.VMEM((slabs, tiles, LANES), F32),
            pltpu.VMEM((slabs, tiles, LANES), F32),
            pltpu.VMEM((devices, LANES), F32),
            pltpu.VMEM((devices, LANES), F32),
            pltpu.VMEM((3, CZ + 3, 16, wide), F32),
            pltpu.VMEM((3, 3, CZ, CX, wide), F32),
            pltpu.VMEM((2, 9, 16, wide), F32),
            pltpu.VMEM((2, 3, CZ + 2, 16, NY), F32),
            pltpu.VMEM((2, CZ + 1, 16, NY), F32),
            pltpu.VMEM((2, slabs, LANES), F32),
            pltpu.VMEM((2, tiles, LANES), F32),
            dma((slabs + tiles,)),
            dma((slabs,)),
            dma((tiles,)),
            dma((3, 3)),
            dma((3, 3)),
            dma((2, 8)),
            dma((2, 8)),
            dma((2, 2, max(slabs, tiles))),
            dma((2, slabs)),
            dma((2, tiles)),
        ],
        compiler_params=pltpu.CompilerParams(collective_id=0, has_side_effects=True),
    )(owner.reshape(1, count), block_base, spline_weights, measured, div_weight, bend_weight)


def solution(mesh):
    placed = (
        P(("slab", "tile"), None),
        P(None, ("slab", "tile")),
        P(None, ("slab", "tile")),
        P(None, ("slab", "tile")),
        P(),
        P(),
    )
    sizes = dict(zip(mesh.axis_names, mesh.devices.shape))
    return jax.shard_map(
        functools.partial(local, sizes["slab"], sizes["tile"]),
        mesh=mesh,
        in_specs=placed,
        out_specs=(P(None, "slab", "tile", None), P(None, "slab", "tile", None)),
        check_vma=False,
    )
```

```python
import functools

import jax
import jax.numpy as jnp
from jax import lax
from jax.experimental import pallas as pl
from jax.experimental.pallas import tpu as pltpu
from jax.sharding import PartitionSpec as P

CZ = 4
CX = 8
NY = 128
CAP = 4
LANES = 128
F32 = jnp.float32
BF16 = jnp.bfloat16
NT = (((1,), (1,)), ((), ()))
NN = (((1,), (0,)), ((), ()))
WIDE = (
    ((2, 1), (6, 1), (8, 3)),
    ((1, 1), (2, 5), (6, 5)),
    ((-1, -1), (0, 3), (0, 3)),
    ((1, -1), (3, 4), (0, 3)),
    ((-1, 1), (0, 3), (7, 4)),
    ((0, 1), (0, 7), (6, 5)),
    ((0, -1), (0, 7), (0, 3)),
    ((2, 0), (6, 1), (0, 6)),
    ((2, 0), (6, 1), (6, 2)),
    ((1, 0), (2, 5), (0, 6)),
    ((1, 0), (2, 5), (6, 5)),
    ((-1, 0), (0, 3), (0, 6)),
    ((-1, 0), (0, 3), (6, 5)),
)
LAST = (
    ((1, 1), (4, 3), (8, 3)),
    ((0, 1), (0, 4), (8, 3)),
    ((1, 0), (4, 3), (0, 6)),
    ((1, 0), (4, 3), (6, 2)),
)
ROUNDS = (WIDE, WIDE, LAST)


def landing(entry):
    (s, t), (z, _), (x, _) = entry
    row = x - CX * t + 2
    return z - CZ * s + 2, row % 8, row // 8


def split(value):
    high = value.astype(BF16)
    return high, (value - high.astype(F32)).astype(BF16)


def product(left, right, dims):
    dot = functools.partial(lax.dot_general, dimension_numbers=dims, preferred_element_type=F32)
    return dot(left[0], right[0]) + (dot(left[0], right[1]) + dot(left[1], right[0]))


def kernel(
    slabs, tiles, owner_in, base_in, spline_in, measured_in, div_in, bend_in,
    solution_ref, residual_ref,
    owner_ref, base_ref, spline_ref, measured_ref, div_ref, bend_ref, load_sem,
    pay, out_rows, by_slab, turned, by_tile,
    partial, field, bent, source, sum_slab, sum_tile,
    pass_send, pass_slab_recv, pass_tile_recv, wide_send, wide_recv,
    sum_send, sum_slab_recv, sum_tile_recv,
    *landed,
):
    landed = (landed[: len(WIDE)], landed[len(WIDE) : 2 * len(WIDE)], landed[2 * len(WIDE) :])
    devices = slabs * tiles
    slab, tile = lax.axis_index("slab"), lax.axis_index("tile")
    count = owner_ref.shape[1]

    barrier = pltpu.get_barrier_semaphore()
    drains = []

    def finish():
        for drain in drains:
            drain()

    def mesh_at(s, t):
        return {"slab": s, "tile": t}

    def other_slab(step):
        return lax.rem(slab + step, slabs)

    def other_tile(step):
        return lax.rem(tile + step, tiles)

    loads = [
        pltpu.make_async_copy(source, target, load_sem.at[number])
        for number, (source, target) in enumerate((
            (owner_in, owner_ref), (base_in, base_ref), (spline_in, spline_ref),
            (measured_in, measured_ref), (div_in, div_ref), (bend_in, bend_ref),
        ))
    ]
    for load in loads:
        load.start()

    for step in range(1, slabs):
        pl.semaphore_signal(barrier, inc=1, device_id=mesh_at(other_slab(step), tile))
    for step in range(1, tiles):
        pl.semaphore_signal(barrier, inc=1, device_id=mesh_at(slab, other_tile(step)))

    for buffers in landed:
        for buffer in buffers:
            buffer[...] = jnp.zeros_like(buffer)

    for load in loads:
        load.wait()

    pay[...] = jnp.zeros_like(pay)
    pay[0:12, :] = spline_ref[...]
    pay[12:15, :] = measured_ref[...]
    pay[15:18, :] = base_ref[...].astype(F32)
    owner = owner_ref[...]
    onehot = (lax.broadcasted_iota(jnp.int32, (devices, count), 0) == owner).astype(F32)
    onehot_b = onehot.astype(BF16)
    earlier = (
        lax.broadcasted_iota(jnp.int32, (count, count), 0)
        < lax.broadcasted_iota(jnp.int32, (count, count), 1)
    ).astype(BF16)
    before = lax.dot_general(onehot_b, earlier, NN, preferred_element_type=F32)
    rank = jnp.sum(onehot * before, axis=0, keepdims=True)
    payload = pay[...]
    slots = jnp.concatenate([jnp.where(rank == k, payload, 0.0) for k in range(CAP)], axis=0)
    high, low = split(slots)
    lowest = (slots - high.astype(F32) - low.astype(F32)).astype(BF16)
    rows = [lax.dot_general(onehot_b, part, NT, preferred_element_type=F32) for part in (high, low, lowest)]
    out_rows[...] = ((rows[0] + rows[1]) + rows[2]).reshape(slabs, tiles, LANES)

    pl.semaphore_wait(barrier, slabs - 1 + tiles - 1)

    for step in range(1, slabs):
        to = other_slab(step)
        copy = pltpu.make_async_remote_copy(
            src_ref=out_rows.at[to], dst_ref=by_slab.at[slab],
            send_sem=pass_send.at[step], recv_sem=pass_slab_recv.at[slab],
            device_id=mesh_at(to, tile),
        )
        copy.start()
        drains.append(copy.wait_send)
    by_slab[slab] = out_rows[slab]
    for step in range(1, slabs):
        origin = other_slab(step)
        pltpu.make_async_remote_copy(
            src_ref=out_rows.at[origin], dst_ref=by_slab.at[origin],
            send_sem=pass_send.at[step], recv_sem=pass_slab_recv.at[origin],
            device_id=mesh_at(origin, tile),
        ).wait_recv()
    for s in range(slabs):
        turned[pl.ds(s, tiles, stride=slabs), :] = by_slab[s]
    for step in range(1, tiles):
        to = other_tile(step)
        copy = pltpu.make_async_remote_copy(
            src_ref=turned.at[pl.ds(to * slabs, slabs)], dst_ref=by_tile.at[pl.ds(tile * slabs, slabs)],
            send_sem=pass_send.at[slabs + step], recv_sem=pass_tile_recv.at[tile],
            device_id=mesh_at(slab, to),
        )
        copy.start()
        drains.append(copy.wait_send)
    by_tile[pl.ds(tile * slabs, slabs), :] = turned[pl.ds(tile * slabs, slabs), :]
    for step in range(1, tiles):
        origin = other_tile(step)
        pltpu.make_async_remote_copy(
            src_ref=turned.at[pl.ds(origin * slabs, slabs)], dst_ref=by_tile.at[pl.ds(origin * slabs, slabs)],
            send_sem=pass_send.at[slabs + step], recv_sem=pass_tile_recv.at[origin],
            device_id=mesh_at(slab, origin),
        ).wait_recv()

    lanes_first = by_tile[...].T
    owned = jnp.concatenate([lanes_first[32 * k : 32 * k + 32] for k in range(CAP)], axis=1)
    total = owned.shape[1]

    def spread_weights(cells, base, first, shift=0):
        offset = lax.broadcasted_iota(jnp.int32, (cells, total), 0).astype(F32) - (owned[base : base + 1] + float(shift))
        result = jnp.zeros((cells, total), F32)
        for step in range(4):
            result = jnp.where(offset == float(step), owned[first + step : first + step + 1], result)
        return result

    weight_z = spread_weights(8, 15, 0)
    weight_x = spread_weights(16, 16, 4, 2)
    weight_y = spread_weights(NY, 17, 8)
    plane = jnp.concatenate([weight_z[z : z + 1] * weight_x for z in range(CZ + 3)], axis=0)
    plane_parts = split(plane)

    def spread(values):
        columns = split(jnp.concatenate([weight_y * values[c] for c in range(3)], axis=0))
        return product(plane_parts, columns, NT).reshape(CZ + 3, 16, 3 * NY)

    def exists(s, t):
        inside = None
        if s:
            inside = (slab < slabs - s) if s > 0 else (slab >= -s)
        if t:
            along = (tile < tiles - t) if t > 0 else (tile >= -t)
            inside = along if inside is None else jnp.logical_and(inside, along)
        return inside

    def wide_copy(turn, number):
        entry = ROUNDS[turn][number]
        (s, t), (z, zs), (x, xs) = entry
        _, row, _ = landing(entry)
        return pltpu.make_async_remote_copy(
            src_ref=partial.at[turn, pl.ds(z, zs), pl.ds(x + 2, xs)],
            dst_ref=landed[turn][number].at[pl.ds(0, zs), pl.ds(row, xs)],
            send_sem=wide_send.at[turn, number], recv_sem=wide_recv.at[turn, number],
            device_id=mesh_at(lax.rem(slab + s + slabs, slabs), lax.rem(tile + t + tiles, tiles)),
        )

    def send_wide(turn):
        for number, entry in enumerate(ROUNDS[turn]):
            start_to(*entry[0], wide_copy(turn, number))

    def start_to(s, t, copy):
        @pl.when(exists(s, t))
        def _():
            copy.start()

        def drain():
            @pl.when(exists(s, t))
            def _():
                copy.wait_send()

        drains.append(drain)

    def wait_wide(turn):
        for number, entry in enumerate(ROUNDS[turn]):

            @pl.when(exists(-entry[0][0], -entry[0][1]))
            def _():
                wide_copy(turn, number).wait_recv()

    def added_up(turn, z):
        halves = [None, None]

        def add(half, value):
            halves[half] = value if halves[half] is None else halves[half] + value

        for number, entry in enumerate(ROUNDS[turn]):
            first, _, half = landing(entry)
            if first <= z < first + entry[1][1]:
                add(half, landed[turn][number][z - first])
        if z >= 2:
            add(0, partial[turn, z - 2, 0:8])
            add(1, partial[turn, z - 2, 8:16])
        return jnp.concatenate(halves, axis=0)

    def in_grid(value, z):
        keep = high_x if z < CZ else high_x & has_high_z
        return jnp.where(keep, value, 0.0)

    def read_samples(turn):
        readings = []
        for c in range(3):
            part = field[turn, 2 : CZ + 5, :, c * NY : (c + 1) * NY].reshape((CZ + 3) * 16, NY).T
            seen = product(split(part), plane_parts, NN)
            readings.append(jnp.sum(seen * weight_y, axis=0, keepdims=True))
        return readings

    lane = lax.broadcasted_iota(jnp.int32, (16, NY), 1)
    place = lax.broadcasted_iota(jnp.int32, (16, NY), 0)
    has_low_z, has_high_z = slab > 0, slab < slabs - 1
    own_x = (place >= 2) & (place < CX + 2)
    inside_x = own_x | ((place == CX + 2) & (tile < tiles - 1)) | ((place == 1) & (tile > 0))
    high_x = jnp.concatenate([(place < CX + 2) | (tile < tiles - 1)] * 3, axis=1)
    own_wide = jnp.concatenate([own_x] * 3, axis=1)

    def after_y(value):
        return jnp.where(lane == NY - 1, 0.0, pltpu.roll(value, NY - 1, 1))

    def before_y(value):
        return jnp.where(lane == 0, 0.0, pltpu.roll(value, 1, 1))

    def after_x(value):
        return pltpu.roll(value, 15, 0)

    def before_x(value):
        return pltpu.roll(value, 1, 0)

    def around(below, middle, above):
        total = (above + below) + (after_x(middle) + before_x(middle))
        return total + (after_y(middle) + before_y(middle)) - 6.0 * middle

    def cell(turn, c, z):
        return field[turn, z + 2, :, c * NY : (c + 1) * NY]

    def inside(value, z):
        keep = inside_x
        if z < 0:
            keep = keep & has_low_z
        if z >= CZ:
            keep = keep & has_high_z
        return jnp.where(keep, value, 0.0)

    def smooth(turn):
        for c in range(3):
            for z in range(-1, CZ + 1):
                value = around(cell(turn, c, z - 1), cell(turn, c, z), cell(turn, c, z + 1))
                bent[turn, c, z + 1] = inside(value, z)
        for z in range(-1, CZ):
            along_z = cell(turn, 0, z + 1) - cell(turn, 0, z)
            along_x = after_x(cell(turn, 1, z)) - cell(turn, 1, z)
            along_y = after_y(cell(turn, 2, z)) - cell(turn, 2, z)
            source[turn, z + 1] = inside(along_z + along_x + along_y, z)

    div_weight = div_ref[0]
    bend_weight = bend_ref[0]

    def penalties(turn, c, z):
        here = source[turn, z + 1]
        if c == 0:
            pushed = source[turn, z] - here
        elif c == 1:
            pushed = before_x(here) - here
        else:
            pushed = before_y(here) - here
        again = around(bent[turn, c, z], bent[turn, c, z + 1], bent[turn, c, z + 2])
        return jnp.where(own_x, div_weight * pushed + bend_weight * again, 0.0)

    def all_penalties(turn):
        return [
            jnp.concatenate([penalties(turn, c, z) for c in range(3)], axis=1) for z in range(CZ)
        ]

    def one(values, keep=None):
        value = functools.reduce(jnp.add, values)
        if keep is not None:
            value = jnp.where(keep, value, 0.0)
        return jnp.sum(jnp.sum(value, axis=0, keepdims=True), axis=1, keepdims=True)

    row_lane = lax.broadcasted_iota(jnp.int32, (1, LANES), 1)

    def sum_copy(turn, stage, step, incoming):
        buffer, size, mine, peer = (
            (sum_slab, slabs, slab, other_slab(step)) if stage == 0 else (sum_tile, tiles, tile, other_tile(step))
        )
        received = sum_slab_recv if stage == 0 else sum_tile_recv
        where = peer if incoming else mine
        return pltpu.make_async_remote_copy(
            src_ref=buffer.at[turn, pl.ds(mine, 1)], dst_ref=buffer.at[turn, pl.ds(where, 1)],
            send_sem=sum_send.at[turn, stage, step], recv_sem=received.at[turn, where],
            device_id=mesh_at(peer, tile) if stage == 0 else mesh_at(slab, peer),
        )

    def start_sum(turn, values):
        row = jnp.zeros((1, LANES), F32)
        for number, value in enumerate(values):
            row = jnp.where(row_lane == number, value, row)
        sum_slab[turn, pl.ds(slab, 1)] = row
        for step in range(1, slabs):
            copy = sum_copy(turn, 0, step, False)
            copy.start()
            drains.append(copy.wait_send)

    def turn_sum(turn):
        for step in range(1, slabs):
            sum_copy(turn, 0, step, True).wait_recv()
        sum_tile[turn, pl.ds(tile, 1)] = jnp.sum(sum_slab[turn], axis=0, keepdims=True)
        for step in range(1, tiles):
            copy = sum_copy(turn, 1, step, False)
            copy.start()
            drains.append(copy.wait_send)

    def end_sum(turn, number):
        for step in range(1, tiles):
            sum_copy(turn, 1, step, True).wait_recv()
        row = jnp.sum(sum_tile[turn], axis=0, keepdims=True)
        return [row[:, i : i + 1] for i in range(number)]

    partial[0] = spread([owned[12 + c : 13 + c] for c in range(3)])
    send_wide(0)
    wait_wide(0)
    for z in range(CZ + 5):
        field[0, z] = in_grid(added_up(0, z), z - 2)
    start = [field[0, z + 2] for z in range(CZ)]

    read_start = read_samples(0)
    smooth(0)

    def energy(readings, sources, bends):
        seen = one([v * v for v in readings])
        pushed = one([v * v for v in sources], own_x)
        again = one([v * v for v in bends], own_x)
        return seen + div_weight * pushed + bend_weight * again

    def own_source(turn):
        return [source[turn, z + 1] for z in range(CZ)]

    def own_bent(turn):
        return [bent[turn, c, z + 1] for c in range(3) for z in range(CZ)]

    square = one([v * v for v in start], own_wide)
    start_sum(0, [square, energy(read_start, own_source(0), own_bent(0))])
    held = all_penalties(0)
    fresh = spread(read_start)
    for z in range(CZ + 3):
        partial[1, z] = fresh[z] + held[z] if z < CZ else fresh[z]
    send_wide(1)
    turn_sum(0)
    wait_wide(1)
    for z in range(CZ + 5):
        field[1, z] = in_grid(added_up(1, z), z - 2)
    image = [field[1, z + 2] for z in range(CZ)]

    read_image = read_samples(1)
    smooth(1)
    norm, curvature = end_sum(0, 2)
    step_size = norm / curvature
    left = [b - step_size * y for b, y in zip(start, image)]
    left_square = one([v * v for v in left], own_wide)
    left_image = one([v * y for v, y in zip(left, image)], own_wide)
    left_energy = energy(
        [a - step_size * b for a, b in zip(read_start, read_image)],
        [a - step_size * b for a, b in zip(own_source(0), own_source(1))],
        [a - step_size * b for a, b in zip(own_bent(0), own_bent(1))],
    )
    start_sum(1, [left_square, left_image, left_energy])
    partial[2] = spread(read_image)
    send_wide(2)
    held = all_penalties(1)
    turn_sum(1)
    wait_wide(2)
    second = [added_up(2, z + 2) + held[z] for z in range(CZ)]
    left_square, left_image, left_energy = end_sum(1, 3)

    ratio = left_square / norm
    bowed = left_energy + 2.0 * ratio * left_image + ratio * ratio * curvature
    step_next = left_square / bowed
    for z in range(CZ):
        direction = left[z] + ratio * start[z]
        pushed = (image[z] - step_size * second[z]) + ratio * image[z]
        answer = step_size * start[z] + step_next * direction
        rest = left[z] - step_next * pushed
        for c in range(3):
            solution_ref[c, z] = answer[2 : CX + 2, c * NY : (c + 1) * NY]
            residual_ref[c, z] = rest[2 : CX + 2, c * NY : (c + 1) * NY]

    finish()


def local(slabs, tiles, owner, block_base, spline_weights, measured, div_weight, bend_weight):
    devices = slabs * tiles
    count = owner.shape[0]
    vmem = pl.BlockSpec(memory_space=pltpu.VMEM)
    dma = pltpu.SemaphoreType.DMA
    wide = 3 * NY
    out = pltpu.VMEM((3, CZ, CX, NY), F32)
    return pl.pallas_call(
        functools.partial(kernel, slabs, tiles),
        out_shape=(out, out),
        in_specs=[pl.BlockSpec(memory_space=pltpu.HBM)] * 6,
        out_specs=(vmem, vmem),
        scratch_shapes=[
            pltpu.VMEM((1, count), jnp.int32),
            pltpu.VMEM((3, count), jnp.int32),
            pltpu.VMEM((12, count), F32),
            pltpu.VMEM((3, count), F32),
            pltpu.SMEM((1,), F32),
            pltpu.SMEM((1,), F32),
            dma((6,)),
            pltpu.VMEM((32, count), F32),
            pltpu.VMEM((slabs, tiles, LANES), F32),
            pltpu.VMEM((slabs, tiles, LANES), F32),
            pltpu.VMEM((devices, LANES), F32),
            pltpu.VMEM((devices, LANES), F32),
            pltpu.VMEM((3, CZ + 3, 16, wide), F32),
            pltpu.VMEM((2, 9, 16, wide), F32),
            pltpu.VMEM((2, 3, CZ + 2, 16, NY), F32),
            pltpu.VMEM((2, CZ + 1, 16, NY), F32),
            pltpu.VMEM((2, slabs, LANES), F32),
            pltpu.VMEM((2, tiles, LANES), F32),
            dma((slabs + tiles,)),
            dma((slabs,)),
            dma((tiles,)),
            dma((3, len(WIDE))),
            dma((3, len(WIDE))),
            dma((2, 2, max(slabs, tiles))),
            dma((2, slabs)),
            dma((2, tiles)),
        ]
        + [pltpu.VMEM((entry[1][1], 8, wide), F32) for entries in ROUNDS for entry in entries],
        compiler_params=pltpu.CompilerParams(collective_id=0, has_side_effects=True),
    )(owner.reshape(1, count), block_base, spline_weights, measured, div_weight, bend_weight)


def solution(mesh):
    placed = (
        P(("slab", "tile"), None),
        P(None, ("slab", "tile")),
        P(None, ("slab", "tile")),
        P(None, ("slab", "tile")),
        P(),
        P(),
    )
    sizes = dict(zip(mesh.axis_names, mesh.devices.shape))
    return jax.shard_map(
        functools.partial(local, sizes["slab"], sizes["tile"]),
        mesh=mesh,
        in_specs=placed,
        out_specs=(P(None, "slab", "tile", None), P(None, "slab", "tile", None)),
        check_vma=False,
    )
```

```python
import functools

import jax
import jax.numpy as jnp
from jax import lax
from jax.experimental import pallas as pl
from jax.experimental.pallas import tpu as pltpu
from jax.sharding import PartitionSpec as P

CZ = 4
CX = 8
NY = 128
CAP = 4
LANES = 128
F32 = jnp.float32
BF16 = jnp.bfloat16
NT = (((1,), (1,)), ((), ()))
NN = (((1,), (0,)), ((), ()))
WIDE = (
    ((2, 1), (6, 1), (8, 3)),
    ((1, 1), (2, 5), (6, 5)),
    ((-1, -1), (0, 3), (0, 3)),
    ((1, -1), (3, 4), (0, 3)),
    ((-1, 1), (0, 3), (7, 4)),
    ((0, 1), (0, 7), (6, 5)),
    ((0, -1), (0, 7), (0, 3)),
    ((2, 0), (6, 1), (0, 6)),
    ((2, 0), (6, 1), (6, 2)),
    ((1, 0), (2, 5), (0, 6)),
    ((1, 0), (2, 5), (6, 5)),
    ((-1, 0), (0, 3), (0, 6)),
    ((-1, 0), (0, 3), (6, 5)),
)
LAST = (
    ((1, 1), (4, 3), (8, 3)),
    ((0, 1), (0, 4), (8, 3)),
    ((1, 0), (4, 3), (0, 6)),
    ((1, 0), (4, 3), (6, 2)),
)
ROUNDS = (WIDE, WIDE, LAST)


def landing(entry):
    (s, t), (z, _), (x, _) = entry
    row = x - CX * t + 2
    return z - CZ * s + 2, row % 8, row // 8


def split(value):
    high = value.astype(BF16)
    return high, (value - high.astype(F32)).astype(BF16)


def product(left, right, dims):
    dot = functools.partial(lax.dot_general, dimension_numbers=dims, preferred_element_type=F32)
    return dot(left[0], right[0]) + (dot(left[0], right[1]) + dot(left[1], right[0]))


def kernel(
    slabs, tiles, owner_in, base_in, spline_in, measured_in, div_in, bend_in,
    solution_ref, residual_ref,
    owner_ref, base_ref, spline_ref, measured_ref, div_ref, bend_ref, load_sem,
    pay, out_rows, by_slab, turned, by_tile,
    partial, field, bent, source,
    pass_send, pass_slab_recv, pass_tile_recv, wide_send, wide_recv,
    sums, sum_sem,
    *landed,
):
    landed = (landed[: len(WIDE)], landed[len(WIDE) : 2 * len(WIDE)], landed[2 * len(WIDE) :])
    devices = slabs * tiles
    slab, tile = lax.axis_index("slab"), lax.axis_index("tile")
    count = owner_ref.shape[1]

    barrier = pltpu.get_barrier_semaphore()
    drains = []

    def finish():
        for drain in drains:
            drain()

    def mesh_at(s, t):
        return {"slab": s, "tile": t}

    def other_slab(step):
        return lax.rem(slab + step, slabs)

    def other_tile(step):
        return lax.rem(tile + step, tiles)

    loads = [
        pltpu.make_async_copy(source, target, load_sem.at[number])
        for number, (source, target) in enumerate((
            (owner_in, owner_ref), (base_in, base_ref), (spline_in, spline_ref),
            (measured_in, measured_ref), (div_in, div_ref), (bend_in, bend_ref),
        ))
    ]
    for load in loads:
        load.start()

    for step in range(1, slabs):
        pl.semaphore_signal(barrier, inc=1, device_id=mesh_at(other_slab(step), tile))
    for step in range(1, tiles):
        pl.semaphore_signal(barrier, inc=1, device_id=mesh_at(slab, other_tile(step)))

    for buffers in landed:
        for buffer in buffers:
            buffer[...] = jnp.zeros_like(buffer)

    for load in loads:
        load.wait()

    pay[...] = jnp.zeros_like(pay)
    pay[0:12, :] = spline_ref[...]
    pay[12:15, :] = measured_ref[...]
    pay[15:18, :] = base_ref[...].astype(F32)
    owner = owner_ref[...]
    onehot = (lax.broadcasted_iota(jnp.int32, (devices, count), 0) == owner).astype(F32)
    onehot_b = onehot.astype(BF16)
    earlier = (
        lax.broadcasted_iota(jnp.int32, (count, count), 0)
        < lax.broadcasted_iota(jnp.int32, (count, count), 1)
    ).astype(BF16)
    before = lax.dot_general(onehot_b, earlier, NN, preferred_element_type=F32)
    rank = jnp.sum(onehot * before, axis=0, keepdims=True)
    payload = pay[...]
    slots = jnp.concatenate([jnp.where(rank == k, payload, 0.0) for k in range(CAP)], axis=0)
    high, low = split(slots)
    lowest = (slots - high.astype(F32) - low.astype(F32)).astype(BF16)
    rows = [lax.dot_general(onehot_b, part, NT, preferred_element_type=F32) for part in (high, low, lowest)]
    out_rows[...] = ((rows[0] + rows[1]) + rows[2]).reshape(slabs, tiles, LANES)

    pl.semaphore_wait(barrier, slabs - 1 + tiles - 1)

    for step in range(1, slabs):
        to = other_slab(step)
        copy = pltpu.make_async_remote_copy(
            src_ref=out_rows.at[to], dst_ref=by_slab.at[slab],
            send_sem=pass_send.at[step], recv_sem=pass_slab_recv.at[slab],
            device_id=mesh_at(to, tile),
        )
        copy.start()
        drains.append(copy.wait_send)
    by_slab[slab] = out_rows[slab]
    for step in range(1, slabs):
        origin = other_slab(step)
        pltpu.make_async_remote_copy(
            src_ref=out_rows.at[origin], dst_ref=by_slab.at[origin],
            send_sem=pass_send.at[step], recv_sem=pass_slab_recv.at[origin],
            device_id=mesh_at(origin, tile),
        ).wait_recv()
    for s in range(slabs):
        turned[pl.ds(s, tiles, stride=slabs), :] = by_slab[s]
    for step in range(1, tiles):
        to = other_tile(step)
        copy = pltpu.make_async_remote_copy(
            src_ref=turned.at[pl.ds(to * slabs, slabs)], dst_ref=by_tile.at[pl.ds(tile * slabs, slabs)],
            send_sem=pass_send.at[slabs + step], recv_sem=pass_tile_recv.at[tile],
            device_id=mesh_at(slab, to),
        )
        copy.start()
        drains.append(copy.wait_send)
    by_tile[pl.ds(tile * slabs, slabs), :] = turned[pl.ds(tile * slabs, slabs), :]
    for step in range(1, tiles):
        origin = other_tile(step)
        pltpu.make_async_remote_copy(
            src_ref=turned.at[pl.ds(origin * slabs, slabs)], dst_ref=by_tile.at[pl.ds(origin * slabs, slabs)],
            send_sem=pass_send.at[slabs + step], recv_sem=pass_tile_recv.at[origin],
            device_id=mesh_at(slab, origin),
        ).wait_recv()

    lanes_first = by_tile[...].T
    owned = jnp.concatenate([lanes_first[32 * k : 32 * k + 32] for k in range(CAP)], axis=1)
    total = owned.shape[1]

    def spread_weights(cells, base, first, shift=0):
        offset = lax.broadcasted_iota(jnp.int32, (cells, total), 0).astype(F32) - (owned[base : base + 1] + float(shift))
        result = jnp.zeros((cells, total), F32)
        for step in range(4):
            result = jnp.where(offset == float(step), owned[first + step : first + step + 1], result)
        return result

    weight_z = spread_weights(8, 15, 0)
    weight_x = spread_weights(16, 16, 4, 2)
    weight_y = spread_weights(NY, 17, 8)
    plane = jnp.concatenate([weight_z[z : z + 1] * weight_x for z in range(CZ + 3)], axis=0)
    plane_parts = split(plane)

    def spread(values):
        columns = split(jnp.concatenate([weight_y * values[c] for c in range(3)], axis=0))
        return product(plane_parts, columns, NT).reshape(CZ + 3, 16, 3 * NY)

    def exists(s, t):
        inside = None
        if s:
            inside = (slab < slabs - s) if s > 0 else (slab >= -s)
        if t:
            along = (tile < tiles - t) if t > 0 else (tile >= -t)
            inside = along if inside is None else jnp.logical_and(inside, along)
        return inside

    def wide_copy(turn, number):
        entry = ROUNDS[turn][number]
        (s, t), (z, zs), (x, xs) = entry
        _, row, _ = landing(entry)
        return pltpu.make_async_remote_copy(
            src_ref=partial.at[turn, pl.ds(z, zs), pl.ds(x + 2, xs)],
            dst_ref=landed[turn][number].at[pl.ds(0, zs), pl.ds(row, xs)],
            send_sem=wide_send.at[turn, number], recv_sem=wide_recv.at[turn, number],
            device_id=mesh_at(lax.rem(slab + s + slabs, slabs), lax.rem(tile + t + tiles, tiles)),
        )

    def send_wide(turn):
        for number, entry in enumerate(ROUNDS[turn]):
            start_to(*entry[0], wide_copy(turn, number))

    def start_to(s, t, copy):
        @pl.when(exists(s, t))
        def _():
            copy.start()

        def drain():
            @pl.when(exists(s, t))
            def _():
                copy.wait_send()

        drains.append(drain)

    def wait_wide(turn):
        for number, entry in enumerate(ROUNDS[turn]):

            @pl.when(exists(-entry[0][0], -entry[0][1]))
            def _():
                wide_copy(turn, number).wait_recv()

    def added_up(turn, z):
        halves = [None, None]

        def add(half, value):
            halves[half] = value if halves[half] is None else halves[half] + value

        for number, entry in enumerate(ROUNDS[turn]):
            first, _, half = landing(entry)
            if first <= z < first + entry[1][1]:
                add(half, landed[turn][number][z - first])
        if z >= 2:
            add(0, partial[turn, z - 2, 0:8])
            add(1, partial[turn, z - 2, 8:16])
        return jnp.concatenate(halves, axis=0)

    def in_grid(value, z):
        keep = high_x if z < CZ else high_x & has_high_z
        return jnp.where(keep, value, 0.0)

    def read_samples(turn):
        readings = []
        for c in range(3):
            part = field[turn, 2 : CZ + 5, :, c * NY : (c + 1) * NY].reshape((CZ + 3) * 16, NY).T
            seen = product(split(part), plane_parts, NN)
            readings.append(jnp.sum(seen * weight_y, axis=0, keepdims=True))
        return readings

    lane = lax.broadcasted_iota(jnp.int32, (16, NY), 1)
    place = lax.broadcasted_iota(jnp.int32, (16, NY), 0)
    has_low_z, has_high_z = slab > 0, slab < slabs - 1
    own_x = (place >= 2) & (place < CX + 2)
    inside_x = own_x | ((place == CX + 2) & (tile < tiles - 1)) | ((place == 1) & (tile > 0))
    high_x = jnp.concatenate([(place < CX + 2) | (tile < tiles - 1)] * 3, axis=1)
    own_wide = jnp.concatenate([own_x] * 3, axis=1)

    def after_y(value):
        return jnp.where(lane == NY - 1, 0.0, pltpu.roll(value, NY - 1, 1))

    def before_y(value):
        return jnp.where(lane == 0, 0.0, pltpu.roll(value, 1, 1))

    def after_x(value):
        return pltpu.roll(value, 15, 0)

    def before_x(value):
        return pltpu.roll(value, 1, 0)

    def around(below, middle, above):
        total = (above + below) + (after_x(middle) + before_x(middle))
        return total + (after_y(middle) + before_y(middle)) - 6.0 * middle

    def cell(turn, c, z):
        return field[turn, z + 2, :, c * NY : (c + 1) * NY]

    def inside(value, z):
        keep = inside_x
        if z < 0:
            keep = keep & has_low_z
        if z >= CZ:
            keep = keep & has_high_z
        return jnp.where(keep, value, 0.0)

    def smooth(turn):
        for c in range(3):
            for z in range(-1, CZ + 1):
                value = around(cell(turn, c, z - 1), cell(turn, c, z), cell(turn, c, z + 1))
                bent[turn, c, z + 1] = inside(value, z)
        for z in range(-1, CZ):
            along_z = cell(turn, 0, z + 1) - cell(turn, 0, z)
            along_x = after_x(cell(turn, 1, z)) - cell(turn, 1, z)
            along_y = after_y(cell(turn, 2, z)) - cell(turn, 2, z)
            source[turn, z + 1] = inside(along_z + along_x + along_y, z)

    div_weight = div_ref[0]
    bend_weight = bend_ref[0]

    def penalties(turn, c, z):
        here = source[turn, z + 1]
        if c == 0:
            pushed = source[turn, z] - here
        elif c == 1:
            pushed = before_x(here) - here
        else:
            pushed = before_y(here) - here
        again = around(bent[turn, c, z], bent[turn, c, z + 1], bent[turn, c, z + 2])
        return jnp.where(own_x, div_weight * pushed + bend_weight * again, 0.0)

    def all_penalties(turn):
        return [
            jnp.concatenate([penalties(turn, c, z) for c in range(3)], axis=1) for z in range(CZ)
        ]

    def one(values, keep=None):
        value = functools.reduce(jnp.add, values)
        if keep is not None:
            value = jnp.where(keep, value, 0.0)
        return jnp.sum(jnp.sum(value, axis=0, keepdims=True), axis=1, keepdims=True)

    row_lane = lax.broadcasted_iota(jnp.int32, (1, LANES), 1)

    def far_first():
        def hops(i, j):
            z, y, x = (i // 2) % 4, j // 4, j % 4
            return sum(min(k, 4 - k) for k in (z, y, x))

        steps = [(i, j) for i in range(slabs) for j in range(tiles) if i or j]
        return sorted(steps, key=lambda step: -hops(*step))

    me = slab * tiles + tile

    def start_sum(values):
        row = jnp.zeros((1, LANES), F32)
        for number, value in enumerate(values):
            row = jnp.where(row_lane == number, value, row)
        sums[pl.ds(me, 1)] = row
        by_step_slab = [other_slab(step) if step else slab for step in range(slabs)]
        by_step_tile = [other_tile(step) if step else tile for step in range(tiles)]
        for i, j in far_first():
            pltpu.make_async_remote_copy(
                src_ref=sums.at[pl.ds(me, 1)], dst_ref=sums.at[pl.ds(me, 1)],
                send_sem=sum_sem.at[0], recv_sem=sum_sem.at[1],
                device_id=mesh_at(by_step_slab[i], by_step_tile[j]),
            ).start()

    def every_wait(number):
        others = sums.at[pl.ds(0, devices - 1)]
        pltpu.make_async_copy(others, others, sum_sem.at[number]).wait()

    def end_sum(number):
        every_wait(1)
        drains.append(lambda: every_wait(0))
        row = jnp.sum(sums[...], axis=0, keepdims=True)
        return [row[:, i : i + 1] for i in range(number)]

    partial[0] = spread([owned[12 + c : 13 + c] for c in range(3)])
    send_wide(0)
    wait_wide(0)
    for z in range(CZ + 5):
        field[0, z] = in_grid(added_up(0, z), z - 2)
    start = [field[0, z + 2] for z in range(CZ)]

    read_start = read_samples(0)
    smooth(0)

    def energy(readings, sources, bends):
        seen = one([v * v for v in readings])
        pushed = one([v * v for v in sources], own_x)
        again = one([v * v for v in bends], own_x)
        return seen + div_weight * pushed + bend_weight * again

    def own_source(turn):
        return [source[turn, z + 1] for z in range(CZ)]

    def own_bent(turn):
        return [bent[turn, c, z + 1] for c in range(3) for z in range(CZ)]

    held = all_penalties(0)
    fresh = spread(read_start)
    for z in range(CZ + 3):
        partial[1, z] = fresh[z] + held[z] if z < CZ else fresh[z]
    send_wide(1)
    square = one([v * v for v in start], own_wide)
    wait_wide(1)
    for z in range(CZ + 5):
        field[1, z] = in_grid(added_up(1, z), z - 2)
    image = [field[1, z + 2] for z in range(CZ)]

    read_image = read_samples(1)
    smooth(1)
    start_sum([
        square,
        one([v * y for v, y in zip(start, image)], own_wide),
        one([y * y for y in image], own_wide),
        energy(read_image, own_source(1), own_bent(1)),
    ])
    partial[2] = spread(read_image)
    send_wide(2)
    held = all_penalties(1)
    wait_wide(2)
    second = [added_up(2, z + 2) + held[z] for z in range(CZ)]
    norm, curvature, image_square, image_energy = end_sum(4)

    step_size = norm / curvature
    left_square = step_size * step_size * image_square - norm
    ratio = left_square / norm
    left_image = curvature - step_size * image_square
    left_energy = left_image - step_size * (image_square - step_size * image_energy)
    bowed = left_energy + 2.0 * ratio * left_image + ratio * ratio * curvature
    step_next = left_square / bowed
    for z in range(CZ):
        left = start[z] - step_size * image[z]
        direction = left + ratio * start[z]
        pushed = (image[z] - step_size * second[z]) + ratio * image[z]
        answer = step_size * start[z] + step_next * direction
        rest = left - step_next * pushed
        for c in range(3):
            solution_ref[c, z] = answer[2 : CX + 2, c * NY : (c + 1) * NY]
            residual_ref[c, z] = rest[2 : CX + 2, c * NY : (c + 1) * NY]

    finish()


def local(slabs, tiles, owner, block_base, spline_weights, measured, div_weight, bend_weight):
    devices = slabs * tiles
    count = owner.shape[0]
    vmem = pl.BlockSpec(memory_space=pltpu.VMEM)
    dma = pltpu.SemaphoreType.DMA
    wide = 3 * NY
    out = pltpu.VMEM((3, CZ, CX, NY), F32)
    return pl.pallas_call(
        functools.partial(kernel, slabs, tiles),
        out_shape=(out, out),
        in_specs=[pl.BlockSpec(memory_space=pltpu.HBM)] * 6,
        out_specs=(vmem, vmem),
        scratch_shapes=[
            pltpu.VMEM((1, count), jnp.int32),
            pltpu.VMEM((3, count), jnp.int32),
            pltpu.VMEM((12, count), F32),
            pltpu.VMEM((3, count), F32),
            pltpu.SMEM((1,), F32),
            pltpu.SMEM((1,), F32),
            dma((6,)),
            pltpu.VMEM((32, count), F32),
            pltpu.VMEM((slabs, tiles, LANES), F32),
            pltpu.VMEM((slabs, tiles, LANES), F32),
            pltpu.VMEM((devices, LANES), F32),
            pltpu.VMEM((devices, LANES), F32),
            pltpu.VMEM((3, CZ + 3, 16, wide), F32),
            pltpu.VMEM((2, 9, 16, wide), F32),
            pltpu.VMEM((2, 3, CZ + 2, 16, NY), F32),
            pltpu.VMEM((2, CZ + 1, 16, NY), F32),
            dma((slabs + tiles,)),
            dma((slabs,)),
            dma((tiles,)),
            dma((3, len(WIDE))),
            dma((3, len(WIDE))),
            pltpu.VMEM((devices, LANES), F32),
            dma((2,)),
        ]
        + [pltpu.VMEM((entry[1][1], 8, wide), F32) for entries in ROUNDS for entry in entries],
        compiler_params=pltpu.CompilerParams(collective_id=0, has_side_effects=True),
    )(owner.reshape(1, count), block_base, spline_weights, measured, div_weight, bend_weight)


def solution(mesh):
    placed = (
        P(("slab", "tile"), None),
        P(None, ("slab", "tile")),
        P(None, ("slab", "tile")),
        P(None, ("slab", "tile")),
        P(),
        P(),
    )
    sizes = dict(zip(mesh.axis_names, mesh.devices.shape))
    return jax.shard_map(
        functools.partial(local, sizes["slab"], sizes["tile"]),
        mesh=mesh,
        in_specs=placed,
        out_specs=(P(None, "slab", "tile", None), P(None, "slab", "tile", None)),
        check_vma=False,
    )
```

```python
import functools

import jax
import jax.numpy as jnp
from jax import lax
from jax.experimental import pallas as pl
from jax.experimental.pallas import tpu as pltpu
from jax.sharding import PartitionSpec as P

CZ = 4
CX = 8
NY = 128
CAP = 4
LANES = 128
F32 = jnp.float32
BF16 = jnp.bfloat16
NT = (((1,), (1,)), ((), ()))
NN = (((1,), (0,)), ((), ()))
WIDE = (
    ((2, 1), (6, 1), (8, 3)),
    ((1, 1), (2, 5), (6, 5)),
    ((-1, -1), (0, 3), (0, 3)),
    ((1, -1), (3, 4), (0, 3)),
    ((-1, 1), (0, 3), (7, 4)),
    ((0, 1), (0, 7), (6, 5)),
    ((0, -1), (0, 7), (0, 3)),
    ((2, 0), (6, 1), (0, 6)),
    ((2, 0), (6, 1), (6, 2)),
    ((1, 0), (2, 5), (0, 6)),
    ((1, 0), (2, 5), (6, 5)),
    ((-1, 0), (0, 3), (0, 6)),
    ((-1, 0), (0, 3), (6, 5)),
)
LAST = (
    ((1, 1), (4, 3), (8, 3)),
    ((0, 1), (0, 4), (8, 3)),
    ((1, 0), (4, 3), (0, 6)),
    ((1, 0), (4, 3), (6, 2)),
)
ROUNDS = (WIDE, WIDE, LAST)


def landing(entry):
    (s, t), (z, _), (x, _) = entry
    row = x - CX * t + 2
    return z - CZ * s + 2, row % 8, row // 8


def split(value):
    high = value.astype(BF16)
    return high, (value - high.astype(F32)).astype(BF16)


def wrapped(value, size):
    return jnp.where(value >= size, value - size, value)


def kernel(
    slabs, tiles, owner_in, base_in, spline_in, measured_in, div_in, bend_in,
    both_ref,
    owner_ref, base_ref, spline_ref, measured_ref, div_ref, bend_ref, load_sem,
    pay, out_rows, by_slab, turned, by_tile,
    partial, field, bent, source,
    pass_send, pass_slab_recv, pass_tile_recv, wide_send, wide_recv,
    sums, sum_sem, row_in,
    *landed,
):
    landed = (landed[: len(WIDE)], landed[len(WIDE) : 2 * len(WIDE)], landed[2 * len(WIDE) :])
    devices = slabs * tiles
    slab, tile = lax.axis_index("slab"), lax.axis_index("tile")
    count = owner_ref.shape[1]

    barrier = pltpu.get_barrier_semaphore()
    drains = []

    def finish():
        for drain in drains:
            drain()

    def mesh_at(s, t):
        return {"slab": s, "tile": t}

    def other_slab(step):
        return wrapped(slab + step, slabs)

    def other_tile(step):
        return wrapped(tile + step, tiles)

    loads = [
        pltpu.make_async_copy(source, target, load_sem.at[number])
        for number, (source, target) in enumerate((
            (owner_in, owner_ref), (base_in, base_ref), (spline_in, spline_ref),
            (measured_in, measured_ref), (div_in, div_ref), (bend_in, bend_ref),
        ))
    ]
    for load in loads:
        load.start()

    across = 4 if tiles > 4 else 2
    column, line = lax.rem(tile, across), lax.div(tile, across)
    lines = tiles // across
    row_mates = [line * across + wrapped(column + step, across) for step in range(1, across)]
    column_mates = [wrapped(tile + step * across, tiles) for step in range(1, lines)]
    for step in range(1, slabs):
        pl.semaphore_signal(barrier, inc=1, device_id=mesh_at(other_slab(step), tile))
    for mate in row_mates + column_mates:
        pl.semaphore_signal(barrier, inc=1, device_id=mesh_at(slab, mate))

    def far(step):
        x, y = step % 4, step // 4
        return -(min(x, 4 - x) + min(y, tiles // 4 - y))

    for buffers in landed:
        for buffer in buffers:
            buffer[...] = jnp.zeros_like(buffer)

    for load in loads:
        load.wait()

    pay[...] = jnp.zeros_like(pay)
    pay[0:12, :] = spline_ref[...]
    pay[12:15, :] = measured_ref[...]
    pay[15:18, :] = base_ref[...].astype(F32)
    owner = owner_ref[...]
    onehot = (lax.broadcasted_iota(jnp.int32, (devices, count), 0) == owner).astype(F32)
    onehot_b = onehot.astype(BF16)
    earlier = (
        lax.broadcasted_iota(jnp.int32, (count, count), 0)
        < lax.broadcasted_iota(jnp.int32, (count, count), 1)
    ).astype(BF16)
    before = lax.dot_general(onehot_b, earlier, NN, preferred_element_type=F32)
    rank = jnp.sum(onehot * before, axis=0, keepdims=True)
    payload = pay[...]
    slots = jnp.concatenate([jnp.where(rank == k, payload, 0.0) for k in range(CAP)], axis=0)
    high, low = split(slots)
    lowest = (slots - high.astype(F32) - low.astype(F32)).astype(BF16)
    rows = [lax.dot_general(onehot_b, part, NT, preferred_element_type=F32) for part in (high, low, lowest)]
    out_rows[...] = ((rows[0] + rows[1]) + rows[2]).reshape(slabs, tiles, LANES)

    pl.semaphore_wait(barrier, slabs - 1 + across - 1 + lines - 1)
    for mate in column_mates:
        pl.semaphore_signal(row_in, inc=1, device_id=mesh_at(slab, mate))

    for step in sorted(range(1, slabs), key=lambda step: -min(step, slabs - step)):
        to = other_slab(step)
        copy = pltpu.make_async_remote_copy(
            src_ref=out_rows.at[to], dst_ref=by_slab.at[slab],
            send_sem=pass_send.at[step], recv_sem=pass_slab_recv.at[slab],
            device_id=mesh_at(to, tile),
        )
        copy.start()
        drains.append(copy.wait_send)
    by_slab[slab] = out_rows[slab]
    for step in range(1, slabs):
        origin = other_slab(step)
        pltpu.make_async_remote_copy(
            src_ref=out_rows.at[origin], dst_ref=by_slab.at[origin],
            send_sem=pass_send.at[step], recv_sem=pass_slab_recv.at[origin],
            device_id=mesh_at(origin, tile),
        ).wait_recv()
    for s in range(slabs):
        turned[pl.ds(s, tiles, stride=slabs), :] = by_slab[s]
    pl.semaphore_wait(row_in, lines - 1)
    for step in sorted(range(1, tiles), key=far):
        to = other_tile(step)
        copy = pltpu.make_async_remote_copy(
            src_ref=turned.at[pl.ds(to * slabs, slabs)], dst_ref=by_tile.at[pl.ds(tile * slabs, slabs)],
            send_sem=pass_send.at[slabs + step], recv_sem=pass_tile_recv.at[tile],
            device_id=mesh_at(slab, to),
        )
        copy.start()
        drains.append(copy.wait_send)
    by_tile[pl.ds(tile * slabs, slabs), :] = turned[pl.ds(tile * slabs, slabs), :]
    for step in range(1, tiles):
        origin = other_tile(step)
        pltpu.make_async_remote_copy(
            src_ref=turned.at[pl.ds(origin * slabs, slabs)], dst_ref=by_tile.at[pl.ds(origin * slabs, slabs)],
            send_sem=pass_send.at[slabs + step], recv_sem=pass_tile_recv.at[origin],
            device_id=mesh_at(slab, origin),
        ).wait_recv()

    lanes_first = by_tile[...].T
    owned = jnp.concatenate([lanes_first[32 * k : 32 * k + 32] for k in range(CAP)], axis=1)
    total = owned.shape[1]

    def spread_weights(cells, base, first, shift=0):
        offset = lax.broadcasted_iota(jnp.int32, (cells, total), 0).astype(F32) - (owned[base : base + 1] + float(shift))
        result = jnp.zeros((cells, total), F32)
        for step in range(4):
            result = jnp.where(offset == float(step), owned[first + step : first + step + 1], result)
        return result

    weight_z = spread_weights(8, 15, 0)
    weight_x = spread_weights(16, 16, 4, 2)
    weight_y = spread_weights(NY, 17, 8)
    plane = jnp.concatenate([weight_z[z : z + 1] * weight_x for z in range(CZ + 3)], axis=0)
    y_high, y_low = split(weight_y)
    y_reading = jnp.concatenate([y_high, y_high, y_low], axis=0)
    y_spreading = jnp.concatenate([y_high, y_high, y_low], axis=1)
    rows = (CZ + 3) * 16

    def spread(values):
        high, low = split(jnp.concatenate([plane * values[c] for c in range(3)], axis=0))
        result = lax.dot_general(
            jnp.concatenate([high, low, high], axis=1), y_spreading, NT, preferred_element_type=F32
        )
        return [
            jnp.concatenate(
                [result[c * rows + z * 16 : c * rows + z * 16 + 16] for c in range(3)], axis=1
            )
            for z in range(CZ + 3)
        ]

    def exists(s, t):
        inside = None
        if s:
            inside = (slab < slabs - s) if s > 0 else (slab >= -s)
        if t:
            along = (tile < tiles - t) if t > 0 else (tile >= -t)
            inside = along if inside is None else jnp.logical_and(inside, along)
        return inside

    def wide_copy(turn, number):
        entry = ROUNDS[turn][number]
        (s, t), (z, zs), (x, xs) = entry
        _, row, _ = landing(entry)
        return pltpu.make_async_remote_copy(
            src_ref=partial.at[turn, pl.ds(z, zs), pl.ds(x + 2, xs)],
            dst_ref=landed[turn][number].at[pl.ds(0, zs), pl.ds(row, xs)],
            send_sem=wide_send.at[turn, number], recv_sem=wide_recv.at[turn, number],
            device_id=mesh_at(wrapped(slab + s % slabs, slabs), wrapped(tile + t % tiles, tiles)),
        )

    def send_wide(turn):
        for number, entry in enumerate(ROUNDS[turn]):
            start_to(*entry[0], wide_copy(turn, number))

    def start_to(s, t, copy):
        @pl.when(exists(s, t))
        def _():
            copy.start()

        def drain():
            @pl.when(exists(s, t))
            def _():
                copy.wait_send()

        drains.append(drain)

    def wait_wide(turn):
        for number, entry in enumerate(ROUNDS[turn]):

            @pl.when(exists(-entry[0][0], -entry[0][1]))
            def _():
                wide_copy(turn, number).wait_recv()

    def added_up(turn, z):
        halves = [None, None]

        def add(half, value):
            halves[half] = value if halves[half] is None else halves[half] + value

        for number, entry in enumerate(ROUNDS[turn]):
            first, _, half = landing(entry)
            if first <= z < first + entry[1][1]:
                add(half, landed[turn][number][z - first])
        if z >= 2:
            add(0, partial[turn, z - 2, 0:8])
            add(1, partial[turn, z - 2, 8:16])
        return jnp.concatenate(halves, axis=0)

    def in_grid(value, z):
        keep = high_x if z < CZ else high_x & has_high_z
        return jnp.where(keep, value, 0.0)

    def read_samples(turn):
        values = jnp.concatenate(
            [
                field[turn, 2 : CZ + 5, :, c * NY : (c + 1) * NY].reshape(rows, NY)
                for c in range(3)
            ],
            axis=0,
        )
        high, low = split(values)
        seen = lax.dot_general(
            jnp.concatenate([high, low, high], axis=1), y_reading, NN, preferred_element_type=F32
        )
        return [
            jnp.sum(seen[c * rows : (c + 1) * rows] * plane, axis=0, keepdims=True) for c in range(3)
        ]

    lane = lax.broadcasted_iota(jnp.int32, (16, NY), 1)
    place = lax.broadcasted_iota(jnp.int32, (16, NY), 0)
    has_low_z, has_high_z = slab > 0, slab < slabs - 1
    own_x = (place >= 2) & (place < CX + 2)
    inside_x = own_x | ((place == CX + 2) & (tile < tiles - 1)) | ((place == 1) & (tile > 0))
    high_x = jnp.concatenate([(place < CX + 2) | (tile < tiles - 1)] * 3, axis=1)
    own_wide = jnp.concatenate([own_x] * 3, axis=1)

    def after_y(value):
        return jnp.where(lane == NY - 1, 0.0, pltpu.roll(value, NY - 1, 1))

    def before_y(value):
        return jnp.where(lane == 0, 0.0, pltpu.roll(value, 1, 1))

    def after_x(value):
        return pltpu.roll(value, 15, 0)

    def before_x(value):
        return pltpu.roll(value, 1, 0)

    def around(below, middle, above):
        total = (above + below) + (after_x(middle) + before_x(middle))
        return total + (after_y(middle) + before_y(middle)) - 6.0 * middle

    def cell(turn, c, z):
        return field[turn, z + 2, :, c * NY : (c + 1) * NY]

    def inside(value, z):
        keep = inside_x
        if z < 0:
            keep = keep & has_low_z
        if z >= CZ:
            keep = keep & has_high_z
        return jnp.where(keep, value, 0.0)

    def smooth(turn, layers):
        for c in range(3):
            for z in layers:
                value = around(cell(turn, c, z - 1), cell(turn, c, z), cell(turn, c, z + 1))
                bent[turn, c, z + 1] = inside(value, z)
        for z in layers:
            if z == CZ:
                continue
            along_z = cell(turn, 0, z + 1) - cell(turn, 0, z)
            along_x = after_x(cell(turn, 1, z)) - cell(turn, 1, z)
            along_y = after_y(cell(turn, 2, z)) - cell(turn, 2, z)
            source[turn, z + 1] = inside(along_z + along_x + along_y, z)

    div_weight = div_ref[0]
    bend_weight = bend_ref[0]

    def penalties(turn, c, z):
        here = source[turn, z + 1]
        if c == 0:
            pushed = source[turn, z] - here
        elif c == 1:
            pushed = before_x(here) - here
        else:
            pushed = before_y(here) - here
        again = around(bent[turn, c, z], bent[turn, c, z + 1], bent[turn, c, z + 2])
        return jnp.where(own_x, div_weight * pushed + bend_weight * again, 0.0)

    def all_penalties(turn):
        return [
            jnp.concatenate([penalties(turn, c, z) for c in range(3)], axis=1) for z in range(CZ)
        ]

    def one(values, keep=None):
        value = functools.reduce(jnp.add, values)
        if keep is not None:
            value = jnp.where(keep, value, 0.0)
        return jnp.sum(jnp.sum(value, axis=0, keepdims=True), axis=1, keepdims=True)

    row_lane = lax.broadcasted_iota(jnp.int32, (1, LANES), 1)

    me = slab * tiles + tile

    def distance(step):
        i, j = step
        return sum(
            min(k, size - k)
            for k, size in ((i // 2, slabs // 2), (j // 4, max(1, tiles // 4)), (j % 4, 4))
        )

    every = [(i, j) for i in range(slabs) for j in range(tiles) if i or j]
    opposite = {(i, j): (-i % slabs, -j % tiles) for i, j in every}
    paired = sorted([step for step in every if step < opposite[step]], key=lambda step: -distance(step))
    alone = [step for step in every if step == opposite[step]]
    middle = len(paired) // 2

    def send_row(i, j):
        pltpu.make_async_remote_copy(
            src_ref=sums.at[pl.ds(me, 1)], dst_ref=sums.at[pl.ds(me, 1)],
            send_sem=sum_sem.at[0], recv_sem=sum_sem.at[1],
            device_id=mesh_at(wrapped(slab + i, slabs), wrapped(tile + j, tiles)),
        ).start()

    def send_rows(steps):
        def body(turn, carry):
            for i, j in steps:
                send_row(
                    jnp.where(turn == 0, i, -i % slabs), jnp.where(turn == 0, j, -j % tiles)
                )
            return carry

        lax.fori_loop(0, 2, body, 0)

    def start_sum(values):
        row = jnp.zeros((1, LANES), F32)
        for number, value in enumerate(values):
            row = jnp.where(row_lane == number, value, row)
        sums[pl.ds(me, 1)] = row
        send_rows(paired[:middle])

    def go_on_sum():
        for step in alone:
            send_row(*step)
        send_rows(paired[middle:])

    def every_wait(number):
        others = sums.at[pl.ds(0, devices - 1)]
        pltpu.make_async_copy(others, others, sum_sem.at[number]).wait()

    def end_sum(number):
        every_wait(0)
        every_wait(1)
        row = jnp.sum(sums[...], axis=0, keepdims=True)
        return [row[:, i : i + 1] for i in range(number)]

    for z, value in enumerate(spread([owned[12 + c : 13 + c] for c in range(3)])):
        partial[0, z] = value
    send_wide(0)
    wait_wide(0)
    for z in range(CZ + 5):
        field[0, z] = in_grid(added_up(0, z), z - 2)
    start = [field[0, z + 2] for z in range(CZ)]

    read_start = read_samples(0)
    smooth(0, range(-1, CZ + 1))

    def energy(readings, sources, bends):
        seen = one([v * v for v in readings])
        pushed = one([v * v for v in sources], own_x)
        again = one([v * v for v in bends], own_x)
        return seen + div_weight * pushed + bend_weight * again

    def own_source(turn):
        return [source[turn, z + 1] for z in range(CZ)]

    def own_bent(turn):
        return [bent[turn, c, z + 1] for c in range(3) for z in range(CZ)]

    held = all_penalties(0)
    fresh = spread(read_start)
    for z in range(CZ + 3):
        partial[1, z] = fresh[z] + held[z] if z < CZ else fresh[z]
    send_wide(1)
    square = one([v * v for v in start], own_wide)
    wait_wide(1)
    for z in range(CZ + 5):
        field[1, z] = in_grid(added_up(1, z), z - 2)
    image = [field[1, z + 2] for z in range(CZ)]

    read_image = read_samples(1)
    smooth(1, range(CZ))
    start_sum([
        square,
        one([v * y for v, y in zip(start, image)], own_wide),
        one([y * y for y in image], own_wide),
        energy(read_image, own_source(1), own_bent(1)),
    ])
    for z, value in enumerate(spread(read_image)):
        partial[2, z] = value
    send_wide(2)
    go_on_sum()
    smooth(1, (-1, CZ))
    held = all_penalties(1)
    wait_wide(2)
    second = [added_up(2, z + 2) + held[z] for z in range(CZ)]
    finish()
    norm, curvature, image_square, image_energy = end_sum(4)

    step_size = norm / curvature
    left_square = step_size * step_size * image_square - norm
    ratio = left_square / norm
    left_image = curvature - step_size * image_square
    left_energy = left_image - step_size * (image_square - step_size * image_energy)
    bowed = left_energy + 2.0 * ratio * left_image + ratio * ratio * curvature
    step_next = left_square / bowed
    for z in range(CZ):
        left = start[z] - step_size * image[z]
        direction = left + ratio * start[z]
        pushed = (image[z] - step_size * second[z]) + ratio * image[z]
        answer = step_size * start[z] + step_next * direction
        rest = left - step_next * pushed
        for c in range(3):
            both_ref[0, c, z] = answer[2 : CX + 2, c * NY : (c + 1) * NY]
            both_ref[1, c, z] = rest[2 : CX + 2, c * NY : (c + 1) * NY]


def local(slabs, tiles, owner, block_base, spline_weights, measured, div_weight, bend_weight):
    devices = slabs * tiles
    count = owner.shape[0]
    vmem = pl.BlockSpec(memory_space=pltpu.VMEM)
    dma = pltpu.SemaphoreType.DMA
    wide = 3 * NY
    out = pltpu.VMEM((2, 3, CZ, CX, NY), F32)
    both = pl.pallas_call(
        functools.partial(kernel, slabs, tiles),
        out_shape=out,
        in_specs=[pl.BlockSpec(memory_space=pltpu.HBM)] * 6,
        out_specs=vmem,
        scratch_shapes=[
            pltpu.VMEM((1, count), jnp.int32),
            pltpu.VMEM((3, count), jnp.int32),
            pltpu.VMEM((12, count), F32),
            pltpu.VMEM((3, count), F32),
            pltpu.SMEM((1,), F32),
            pltpu.SMEM((1,), F32),
            dma((6,)),
            pltpu.VMEM((32, count), F32),
            pltpu.VMEM((slabs, tiles, LANES), F32),
            pltpu.VMEM((slabs, tiles, LANES), F32),
            pltpu.VMEM((devices, LANES), F32),
            pltpu.VMEM((devices, LANES), F32),
            pltpu.VMEM((3, CZ + 3, 16, wide), F32),
            pltpu.VMEM((2, 9, 16, wide), F32),
            pltpu.VMEM((2, 3, CZ + 2, 16, NY), F32),
            pltpu.VMEM((2, CZ + 1, 16, NY), F32),
            dma((slabs + tiles,)),
            dma((slabs,)),
            dma((tiles,)),
            dma((3, len(WIDE))),
            dma((3, len(WIDE))),
            pltpu.VMEM((devices, LANES), F32),
            dma((2,)),
            pltpu.SemaphoreType.REGULAR,
        ]
        + [pltpu.VMEM((entry[1][1], 8, wide), F32) for entries in ROUNDS for entry in entries],
        compiler_params=pltpu.CompilerParams(collective_id=0, has_side_effects=True),
    )(owner.reshape(1, count), block_base, spline_weights, measured, div_weight, bend_weight)
    return both[0], both[1]


def solution(mesh):
    placed = (
        P(("slab", "tile"), None),
        P(None, ("slab", "tile")),
        P(None, ("slab", "tile")),
        P(None, ("slab", "tile")),
        P(),
        P(),
    )
    sizes = dict(zip(mesh.axis_names, mesh.devices.shape))
    return jax.shard_map(
        functools.partial(local, sizes["slab"], sizes["tile"]),
        mesh=mesh,
        in_specs=placed,
        out_specs=(P(None, "slab", "tile", None), P(None, "slab", "tile", None)),
        check_vma=False,
    )
```

```python
import functools

import jax
import jax.numpy as jnp
from jax import lax
from jax.experimental import pallas as pl
from jax.experimental.pallas import tpu as pltpu
from jax.sharding import PartitionSpec as P

CZ = 4
CX = 8
NY = 128
CAP = 4
LANES = 128
F32 = jnp.float32
BF16 = jnp.bfloat16
NT = (((1,), (1,)), ((), ()))
NN = (((1,), (0,)), ((), ()))
WIDE = (
    ((2, 1), (6, 1), (8, 3)),
    ((1, 1), (2, 5), (6, 5)),
    ((-1, -1), (0, 3), (0, 3)),
    ((1, -1), (3, 4), (0, 3)),
    ((-1, 1), (0, 3), (7, 4)),
    ((0, 1), (0, 7), (6, 5)),
    ((0, -1), (0, 7), (0, 3)),
    ((2, 0), (6, 1), (0, 6)),
    ((2, 0), (6, 1), (6, 2)),
    ((1, 0), (2, 5), (0, 6)),
    ((1, 0), (2, 5), (6, 5)),
    ((-1, 0), (0, 3), (0, 6)),
    ((-1, 0), (0, 3), (6, 5)),
)
LAST = (
    ((1, 1), (4, 3), (8, 3)),
    ((0, 1), (0, 4), (8, 3)),
    ((1, 0), (4, 3), (0, 6)),
    ((1, 0), (4, 3), (6, 2)),
)
ROUNDS = (WIDE, WIDE, LAST)


def landing(entry):
    (s, t), (z, _), (x, _) = entry
    row = x - CX * t + 2
    return z - CZ * s + 2, row % 8, row // 8


def split(value):
    high = value.astype(BF16)
    return high, (value - high.astype(F32)).astype(BF16)


def wrapped(value, size):
    return jnp.where(value >= size, value - size, value)


def kernel(
    slabs, tiles, owner_in, base_in, spline_in, measured_in, div_in, bend_in,
    both_ref,
    owner_ref, base_ref, spline_ref, measured_ref, div_ref, bend_ref, load_sem,
    pay, out_rows, by_slab, turned, by_tile,
    partial, field, bent, source,
    pass_send, pass_slab_recv, pass_tile_recv, wide_send, wide_recv,
    sums, sum_sem, row_in,
    *landed,
):
    landed = (landed[: len(WIDE)], landed[len(WIDE) : 2 * len(WIDE)], landed[2 * len(WIDE) :])
    devices = slabs * tiles
    slab, tile = lax.axis_index("slab"), lax.axis_index("tile")
    count = owner_ref.shape[1]

    barrier = pltpu.get_barrier_semaphore()
    drains = []

    def finish():
        for drain in drains:
            drain()

    def mesh_at(s, t):
        return {"slab": s, "tile": t}

    def other_slab(step):
        return wrapped(slab + step, slabs)

    def other_tile(step):
        return wrapped(tile + step, tiles)

    loads = [
        pltpu.make_async_copy(source, target, load_sem.at[number])
        for number, (source, target) in enumerate((
            (owner_in, owner_ref), (base_in, base_ref), (spline_in, spline_ref),
            (measured_in, measured_ref), (div_in, div_ref), (bend_in, bend_ref),
        ))
    ]
    for load in loads:
        load.start()

    across = 4 if tiles > 4 else 2
    column, line = lax.rem(tile, across), lax.div(tile, across)
    lines = tiles // across
    row_mates = [line * across + wrapped(column + step, across) for step in range(1, across)]
    column_mates = [wrapped(tile + step * across, tiles) for step in range(1, lines)]
    for step in range(1, slabs):
        pl.semaphore_signal(barrier, inc=1, device_id=mesh_at(other_slab(step), tile))
    for mate in row_mates + column_mates:
        pl.semaphore_signal(barrier, inc=1, device_id=mesh_at(slab, mate))

    def far(step):
        x, y = step % 4, step // 4
        return -(min(x, 4 - x) + min(y, tiles // 4 - y))

    for buffers in landed:
        for buffer in buffers:
            buffer[...] = jnp.zeros_like(buffer)

    for load in loads:
        load.wait()

    pay[...] = jnp.zeros_like(pay)
    pay[0:12, :] = spline_ref[...]
    pay[12:15, :] = measured_ref[...]
    pay[15:18, :] = base_ref[...].astype(F32)
    owner = owner_ref[...]
    onehot = (lax.broadcasted_iota(jnp.int32, (devices, count), 0) == owner).astype(F32)
    onehot_b = onehot.astype(BF16)
    earlier = (
        lax.broadcasted_iota(jnp.int32, (count, count), 0)
        < lax.broadcasted_iota(jnp.int32, (count, count), 1)
    ).astype(BF16)
    before = lax.dot_general(onehot_b, earlier, NN, preferred_element_type=F32)
    rank = jnp.sum(onehot * before, axis=0, keepdims=True)
    payload = pay[...]
    slots = jnp.concatenate([jnp.where(rank == k, payload, 0.0) for k in range(CAP)], axis=0)
    high, low = split(slots)
    lowest = (slots - high.astype(F32) - low.astype(F32)).astype(BF16)
    rows = [lax.dot_general(onehot_b, part, NT, preferred_element_type=F32) for part in (high, low, lowest)]
    out_rows[...] = ((rows[0] + rows[1]) + rows[2]).reshape(slabs, tiles, LANES)

    pl.semaphore_wait(barrier, slabs - 1 + across - 1 + lines - 1)
    for mate in column_mates:
        pl.semaphore_signal(row_in, inc=1, device_id=mesh_at(slab, mate))

    for step in sorted(range(1, slabs), key=lambda step: -min(step, slabs - step)):
        to = other_slab(step)
        copy = pltpu.make_async_remote_copy(
            src_ref=out_rows.at[to], dst_ref=by_slab.at[slab],
            send_sem=pass_send.at[step], recv_sem=pass_slab_recv.at[slab],
            device_id=mesh_at(to, tile),
        )
        copy.start()
        drains.append(copy.wait_send)
    by_slab[slab] = out_rows[slab]
    for step in range(1, slabs):
        origin = other_slab(step)
        pltpu.make_async_remote_copy(
            src_ref=out_rows.at[origin], dst_ref=by_slab.at[origin],
            send_sem=pass_send.at[step], recv_sem=pass_slab_recv.at[origin],
            device_id=mesh_at(origin, tile),
        ).wait_recv()
    for s in range(slabs):
        turned[pl.ds(s, tiles, stride=slabs), :] = by_slab[s]
    pl.semaphore_wait(row_in, lines - 1)
    for step in sorted(range(1, tiles), key=far):
        to = other_tile(step)
        copy = pltpu.make_async_remote_copy(
            src_ref=turned.at[pl.ds(to * slabs, slabs)], dst_ref=by_tile.at[pl.ds(tile * slabs, slabs)],
            send_sem=pass_send.at[slabs + step], recv_sem=pass_tile_recv.at[tile],
            device_id=mesh_at(slab, to),
        )
        copy.start()
        drains.append(copy.wait_send)
    by_tile[pl.ds(tile * slabs, slabs), :] = turned[pl.ds(tile * slabs, slabs), :]
    for step in range(1, tiles):
        origin = other_tile(step)
        pltpu.make_async_remote_copy(
            src_ref=turned.at[pl.ds(origin * slabs, slabs)], dst_ref=by_tile.at[pl.ds(origin * slabs, slabs)],
            send_sem=pass_send.at[slabs + step], recv_sem=pass_tile_recv.at[origin],
            device_id=mesh_at(slab, origin),
        ).wait_recv()

    lanes_first = by_tile[...].T
    owned = jnp.concatenate([lanes_first[32 * k : 32 * k + 32] for k in range(CAP)], axis=1)
    total = owned.shape[1]

    def spread_weights(cells, base, first, shift=0):
        offset = lax.broadcasted_iota(jnp.int32, (cells, total), 0).astype(F32) - (owned[base : base + 1] + float(shift))
        result = jnp.zeros((cells, total), F32)
        for step in range(4):
            result = jnp.where(offset == float(step), owned[first + step : first + step + 1], result)
        return result

    weight_z = spread_weights(8, 15, 0)
    weight_x = spread_weights(16, 16, 4, 2)
    weight_y = spread_weights(NY, 17, 8)
    plane = jnp.concatenate([weight_z[z : z + 1] * weight_x for z in range(CZ + 3)], axis=0)
    y_high, y_low = split(weight_y)
    y_reading = jnp.concatenate([y_high, y_high, y_low], axis=0)
    y_spreading = jnp.concatenate([y_high, y_high, y_low], axis=1)
    rows = (CZ + 3) * 16

    def spread(values):
        high, low = split(jnp.concatenate([plane * values[c] for c in range(3)], axis=0))
        result = lax.dot_general(
            jnp.concatenate([high, low, high], axis=1), y_spreading, NT, preferred_element_type=F32
        )
        return [
            jnp.concatenate(
                [result[c * rows + z * 16 : c * rows + z * 16 + 16] for c in range(3)], axis=1
            )
            for z in range(CZ + 3)
        ]

    def exists(s, t):
        inside = None
        if s:
            inside = (slab < slabs - s) if s > 0 else (slab >= -s)
        if t:
            along = (tile < tiles - t) if t > 0 else (tile >= -t)
            inside = along if inside is None else jnp.logical_and(inside, along)
        return inside

    def wide_copy(turn, number):
        entry = ROUNDS[turn][number]
        (s, t), (z, zs), (x, xs) = entry
        _, row, _ = landing(entry)
        return pltpu.make_async_remote_copy(
            src_ref=partial.at[turn, pl.ds(z, zs), pl.ds(x + 2, xs)],
            dst_ref=landed[turn][number].at[pl.ds(0, zs), pl.ds(row, xs)],
            send_sem=wide_send.at[turn, number], recv_sem=wide_recv.at[turn, number],
            device_id=mesh_at(wrapped(slab + s % slabs, slabs), wrapped(tile + t % tiles, tiles)),
        )

    def send_wide(turn):
        for number, entry in enumerate(ROUNDS[turn]):
            start_to(*entry[0], wide_copy(turn, number))

    def start_to(s, t, copy):
        @pl.when(exists(s, t))
        def _():
            copy.start()

        def drain():
            @pl.when(exists(s, t))
            def _():
                copy.wait_send()

        drains.append(drain)

    def wait_wide(turn):
        for number, entry in enumerate(ROUNDS[turn]):

            @pl.when(exists(-entry[0][0], -entry[0][1]))
            def _():
                wide_copy(turn, number).wait_recv()

    def added_up(turn, z):
        halves = [None, None]

        def add(half, value):
            halves[half] = value if halves[half] is None else halves[half] + value

        for number, entry in enumerate(ROUNDS[turn]):
            first, _, half = landing(entry)
            if first <= z < first + entry[1][1]:
                add(half, landed[turn][number][z - first])
        if z >= 2:
            add(0, partial[turn, z - 2, 0:8])
            add(1, partial[turn, z - 2, 8:16])
        return jnp.concatenate(halves, axis=0)

    def in_grid(value, z):
        keep = high_x if z < CZ else high_x & has_high_z
        return jnp.where(keep, value, 0.0)

    def read_samples(turn):
        values = jnp.concatenate(
            [
                field[turn, 2 : CZ + 5, :, c * NY : (c + 1) * NY].reshape(rows, NY)
                for c in range(3)
            ],
            axis=0,
        )
        high, low = split(values)
        seen = lax.dot_general(
            jnp.concatenate([high, low, high], axis=1), y_reading, NN, preferred_element_type=F32
        )
        return [
            jnp.sum(seen[c * rows : (c + 1) * rows] * plane, axis=0, keepdims=True) for c in range(3)
        ]

    lane = lax.broadcasted_iota(jnp.int32, (16, NY), 1)
    place = lax.broadcasted_iota(jnp.int32, (16, NY), 0)
    has_low_z, has_high_z = slab > 0, slab < slabs - 1
    own_x = (place >= 2) & (place < CX + 2)
    inside_x = own_x | ((place == CX + 2) & (tile < tiles - 1)) | ((place == 1) & (tile > 0))
    high_x = jnp.concatenate([(place < CX + 2) | (tile < tiles - 1)] * 3, axis=1)
    own_wide = jnp.concatenate([own_x] * 3, axis=1)

    def after_y(value):
        return jnp.where(lane == NY - 1, 0.0, pltpu.roll(value, NY - 1, 1))

    def before_y(value):
        return jnp.where(lane == 0, 0.0, pltpu.roll(value, 1, 1))

    def after_x(value):
        return pltpu.roll(value, 15, 0)

    def before_x(value):
        return pltpu.roll(value, 1, 0)

    def around(below, middle, above):
        total = (above + below) + (after_x(middle) + before_x(middle))
        return total + (after_y(middle) + before_y(middle)) - 6.0 * middle

    def cell(turn, c, z):
        return field[turn, z + 2, :, c * NY : (c + 1) * NY]

    def inside(value, z):
        keep = inside_x
        if z < 0:
            keep = keep & has_low_z
        if z >= CZ:
            keep = keep & has_high_z
        return jnp.where(keep, value, 0.0)

    def smooth(turn, layers):
        for c in range(3):
            for z in layers:
                value = around(cell(turn, c, z - 1), cell(turn, c, z), cell(turn, c, z + 1))
                bent[turn, c, z + 1] = inside(value, z)
        for z in layers:
            if z == CZ:
                continue
            along_z = cell(turn, 0, z + 1) - cell(turn, 0, z)
            along_x = after_x(cell(turn, 1, z)) - cell(turn, 1, z)
            along_y = after_y(cell(turn, 2, z)) - cell(turn, 2, z)
            source[turn, z + 1] = inside(along_z + along_x + along_y, z)

    div_weight = div_ref[0]
    bend_weight = bend_ref[0]

    def penalties(turn, c, z):
        here = source[turn, z + 1]
        if c == 0:
            pushed = source[turn, z] - here
        elif c == 1:
            pushed = before_x(here) - here
        else:
            pushed = before_y(here) - here
        again = around(bent[turn, c, z], bent[turn, c, z + 1], bent[turn, c, z + 2])
        return jnp.where(own_x, div_weight * pushed + bend_weight * again, 0.0)

    def all_penalties(turn):
        return [
            jnp.concatenate([penalties(turn, c, z) for c in range(3)], axis=1) for z in range(CZ)
        ]

    def one(values, keep=None):
        value = functools.reduce(jnp.add, values)
        if keep is not None:
            value = jnp.where(keep, value, 0.0)
        return jnp.sum(jnp.sum(value, axis=0, keepdims=True), axis=1, keepdims=True)

    row_lane = lax.broadcasted_iota(jnp.int32, (1, LANES), 1)

    me = slab * tiles + tile

    def distance(step):
        i, j = step
        return sum(
            min(k, size - k)
            for k, size in ((i // 2, slabs // 2), (j // 4, max(1, tiles // 4)), (j % 4, 4))
        )

    every = [(i, j) for i in range(slabs) for j in range(tiles) if i or j]
    opposite = {(i, j): (-i % slabs, -j % tiles) for i, j in every}
    paired = sorted([step for step in every if step < opposite[step]], key=lambda step: -distance(step))
    alone = [step for step in every if step == opposite[step]]
    middle = len(paired) // 2

    def send_row(i, j):
        pltpu.make_async_remote_copy(
            src_ref=sums.at[pl.ds(me, 1)], dst_ref=sums.at[pl.ds(me, 1)],
            send_sem=sum_sem.at[0], recv_sem=sum_sem.at[1],
            device_id=mesh_at(wrapped(slab + i, slabs), wrapped(tile + j, tiles)),
        ).start()

    def send_rows(steps):
        def body(turn, carry):
            for i, j in steps:
                send_row(
                    jnp.where(turn == 0, i, -i % slabs), jnp.where(turn == 0, j, -j % tiles)
                )
            return carry

        lax.fori_loop(0, 2, body, 0)

    def start_sum(values):
        row = jnp.zeros((1, LANES), F32)
        for number, value in enumerate(values):
            row = jnp.where(row_lane == number, value, row)
        sums[pl.ds(me, 1)] = row
        send_rows(paired[:middle])
        for step in alone:
            send_row(*step)
        send_rows(paired[middle:])

    def every_wait(number):
        others = sums.at[pl.ds(0, devices - 1)]
        pltpu.make_async_copy(others, others, sum_sem.at[number]).wait()

    def end_sum(number):
        every_wait(0)
        every_wait(1)
        row = jnp.sum(sums[...], axis=0, keepdims=True)
        return [row[:, i : i + 1] for i in range(number)]

    for z, value in enumerate(spread([owned[12 + c : 13 + c] for c in range(3)])):
        partial[0, z] = value
    send_wide(0)
    wait_wide(0)
    for z in range(CZ + 5):
        field[0, z] = in_grid(added_up(0, z), z - 2)
    start = [field[0, z + 2] for z in range(CZ)]

    read_start = read_samples(0)
    smooth(0, range(-1, CZ + 1))

    def energy(readings, sources, bends):
        seen = one([v * v for v in readings])
        pushed = one([v * v for v in sources], own_x)
        again = one([v * v for v in bends], own_x)
        return seen + div_weight * pushed + bend_weight * again

    def own_source(turn):
        return [source[turn, z + 1] for z in range(CZ)]

    def own_bent(turn):
        return [bent[turn, c, z + 1] for c in range(3) for z in range(CZ)]

    held = all_penalties(0)
    fresh = spread(read_start)
    for z in range(CZ + 3):
        partial[1, z] = fresh[z] + held[z] if z < CZ else fresh[z]
    send_wide(1)
    square = one([v * v for v in start], own_wide)
    wait_wide(1)
    for z in range(CZ + 5):
        field[1, z] = in_grid(added_up(1, z), z - 2)
    image = [field[1, z + 2] for z in range(CZ)]

    read_image = read_samples(1)
    smooth(1, range(CZ))
    start_sum([
        square,
        one([v * y for v, y in zip(start, image)], own_wide),
        one([y * y for y in image], own_wide),
        energy(read_image, own_source(1), own_bent(1)),
    ])
    for z, value in enumerate(spread(read_image)):
        partial[2, z] = value
    send_wide(2)
    smooth(1, (-1, CZ))
    held = all_penalties(1)
    wait_wide(2)
    second = [added_up(2, z + 2) + held[z] for z in range(CZ)]
    finish()
    norm, curvature, image_square, image_energy = end_sum(4)

    step_size = norm / curvature
    left_square = step_size * step_size * image_square - norm
    ratio = left_square / norm
    left_image = curvature - step_size * image_square
    left_energy = left_image - step_size * (image_square - step_size * image_energy)
    bowed = left_energy + 2.0 * ratio * left_image + ratio * ratio * curvature
    step_next = left_square / bowed
    forward = step_size + step_next * (1.0 + ratio)
    backward = step_size * step_next
    for z in range(CZ):
        answer = forward * start[z] - backward * image[z]
        rest = (start[z] - forward * image[z]) + backward * second[z]
        for c in range(3):
            both_ref[0, c, z] = answer[2 : CX + 2, c * NY : (c + 1) * NY]
            both_ref[1, c, z] = rest[2 : CX + 2, c * NY : (c + 1) * NY]


def local(slabs, tiles, owner, block_base, spline_weights, measured, div_weight, bend_weight):
    devices = slabs * tiles
    count = owner.shape[0]
    vmem = pl.BlockSpec(memory_space=pltpu.VMEM)
    dma = pltpu.SemaphoreType.DMA
    wide = 3 * NY
    out = pltpu.VMEM((2, 3, CZ, CX, NY), F32)
    both = pl.pallas_call(
        functools.partial(kernel, slabs, tiles),
        out_shape=out,
        in_specs=[pl.BlockSpec(memory_space=pltpu.HBM)] * 6,
        out_specs=vmem,
        scratch_shapes=[
            pltpu.VMEM((1, count), jnp.int32),
            pltpu.VMEM((3, count), jnp.int32),
            pltpu.VMEM((12, count), F32),
            pltpu.VMEM((3, count), F32),
            pltpu.SMEM((1,), F32),
            pltpu.SMEM((1,), F32),
            dma((6,)),
            pltpu.VMEM((32, count), F32),
            pltpu.VMEM((slabs, tiles, LANES), F32),
            pltpu.VMEM((slabs, tiles, LANES), F32),
            pltpu.VMEM((devices, LANES), F32),
            pltpu.VMEM((devices, LANES), F32),
            pltpu.VMEM((3, CZ + 3, 16, wide), F32),
            pltpu.VMEM((2, 9, 16, wide), F32),
            pltpu.VMEM((2, 3, CZ + 2, 16, NY), F32),
            pltpu.VMEM((2, CZ + 1, 16, NY), F32),
            dma((slabs + tiles,)),
            dma((slabs,)),
            dma((tiles,)),
            dma((3, len(WIDE))),
            dma((3, len(WIDE))),
            pltpu.VMEM((devices, LANES), F32),
            dma((2,)),
            pltpu.SemaphoreType.REGULAR,
        ]
        + [pltpu.VMEM((entry[1][1], 8, wide), F32) for entries in ROUNDS for entry in entries],
        compiler_params=pltpu.CompilerParams(collective_id=0, has_side_effects=True),
    )(owner.reshape(1, count), block_base, spline_weights, measured, div_weight, bend_weight)
    return both[0], both[1]


def solution(mesh):
    placed = (
        P(("slab", "tile"), None),
        P(None, ("slab", "tile")),
        P(None, ("slab", "tile")),
        P(None, ("slab", "tile")),
        P(),
        P(),
    )
    sizes = dict(zip(mesh.axis_names, mesh.devices.shape))
    return jax.shard_map(
        functools.partial(local, sizes["slab"], sizes["tile"]),
        mesh=mesh,
        in_specs=placed,
        out_specs=(P(None, "slab", "tile", None), P(None, "slab", "tile", None)),
        check_vma=False,
    )
```

```python
import functools
import itertools

import jax
import jax.numpy as jnp
from jax import lax
from jax.experimental import pallas as pl
from jax.experimental.pallas import tpu as pltpu
from jax.sharding import PartitionSpec as P

CZ = 4
CX = 8
NY = 128
CAP = 4
LANES = 128
F32 = jnp.float32
BF16 = jnp.bfloat16
NT = (((1,), (1,)), ((), ()))
NN = (((1,), (0,)), ((), ()))
WIDE = (
    ((2, 1), (6, 1), (8, 3)),
    ((1, 1), (2, 5), (6, 5)),
    ((-1, -1), (0, 3), (0, 3)),
    ((1, -1), (3, 4), (0, 3)),
    ((-1, 1), (0, 3), (7, 4)),
    ((0, 1), (0, 7), (6, 5)),
    ((0, -1), (0, 7), (0, 3)),
    ((2, 0), (6, 1), (0, 6)),
    ((2, 0), (6, 1), (6, 2)),
    ((1, 0), (2, 5), (0, 6)),
    ((1, 0), (2, 5), (6, 5)),
    ((-1, 0), (0, 3), (0, 6)),
    ((-1, 0), (0, 3), (6, 5)),
)
LAST = (
    ((1, 1), (4, 3), (8, 3)),
    ((0, 1), (0, 4), (8, 3)),
    ((1, 0), (4, 3), (0, 6)),
    ((1, 0), (4, 3), (6, 2)),
)
ROUNDS = (WIDE, WIDE, LAST)


def landing(entry):
    (s, t), (z, _), (x, _) = entry
    row = x - CX * t + 2
    return z - CZ * s + 2, row % 8, row // 8


def split(value):
    high = value.astype(BF16)
    return high, (value - high.astype(F32)).astype(BF16)


def wrapped(value, size):
    return jnp.where(value >= size, value - size, value)


def kernel(
    slabs, tiles, owner_in, base_in, spline_in, measured_in, div_in, bend_in,
    both_ref,
    owner_ref, base_ref, spline_ref, measured_ref, div_ref, bend_ref, load_sem,
    pay, out_rows, by_slab, turned, by_tile,
    partial, field, bent, source,
    pass_send, pass_slab_recv, pass_tile_recv, wide_send, wide_recv,
    sums, sum_sem, row_in,
    *landed,
):
    landed = (landed[: len(WIDE)], landed[len(WIDE) : 2 * len(WIDE)], landed[2 * len(WIDE) :])
    devices = slabs * tiles
    slab, tile = lax.axis_index("slab"), lax.axis_index("tile")
    count = owner_ref.shape[1]

    barrier = pltpu.get_barrier_semaphore()
    drains = []

    def finish():
        for drain in drains:
            drain()

    def mesh_at(s, t):
        return {"slab": s, "tile": t}

    def other_slab(step):
        return wrapped(slab + step, slabs)

    def other_tile(step):
        return wrapped(tile + step, tiles)

    across = 4 if tiles > 4 else 2
    column, line = lax.rem(tile, across), lax.div(tile, across)
    lines = tiles // across
    row_mates = [line * across + wrapped(column + step, across) for step in range(1, across)]
    column_mates = [wrapped(tile + step * across, tiles) for step in range(1, lines)]
    for step in sorted(range(1, slabs), key=lambda step: -min(step, slabs - step)):
        pl.semaphore_signal(barrier, inc=1, device_id=mesh_at(other_slab(step), tile))
    for mate in row_mates + column_mates:
        pl.semaphore_signal(barrier, inc=1, device_id=mesh_at(slab, mate))

    loads = [
        pltpu.make_async_copy(source, target, load_sem.at[number])
        for number, (source, target) in enumerate((
            (owner_in, owner_ref), (base_in, base_ref), (spline_in, spline_ref),
            (measured_in, measured_ref), (div_in, div_ref), (bend_in, bend_ref),
        ))
    ]
    for load in loads:
        load.start()

    def far(step):
        x, y = step % 4, step // 4
        return -(min(x, 4 - x) + min(y, tiles // 4 - y))

    for buffers in landed:
        for buffer in buffers:
            buffer[...] = jnp.zeros_like(buffer)

    for load in loads:
        load.wait()

    pay[...] = jnp.zeros_like(pay)
    pay[0:12, :] = spline_ref[...]
    pay[12:15, :] = measured_ref[...]
    pay[15:18, :] = base_ref[...].astype(F32)
    owner = owner_ref[...]
    onehot = (lax.broadcasted_iota(jnp.int32, (devices, count), 0) == owner).astype(F32)
    onehot_b = onehot.astype(BF16)
    earlier = (
        lax.broadcasted_iota(jnp.int32, (count, count), 0)
        < lax.broadcasted_iota(jnp.int32, (count, count), 1)
    ).astype(BF16)
    before = lax.dot_general(onehot_b, earlier, NN, preferred_element_type=F32)
    rank = jnp.sum(onehot * before, axis=0, keepdims=True)
    payload = pay[...]
    slots = jnp.concatenate([jnp.where(rank == k, payload, 0.0) for k in range(CAP)], axis=0)
    high, low = split(slots)
    lowest = (slots - high.astype(F32) - low.astype(F32)).astype(BF16)
    rows = [lax.dot_general(onehot_b, part, NT, preferred_element_type=F32) for part in (high, low, lowest)]
    out_rows[...] = ((rows[0] + rows[1]) + rows[2]).reshape(slabs, tiles, LANES)

    pl.semaphore_wait(barrier, slabs - 1 + across - 1 + lines - 1)
    for mate in column_mates:
        pl.semaphore_signal(row_in, inc=1, device_id=mesh_at(slab, mate))

    for step in sorted(range(1, slabs), key=lambda step: -min(step, slabs - step)):
        to = other_slab(step)
        copy = pltpu.make_async_remote_copy(
            src_ref=out_rows.at[to], dst_ref=by_slab.at[slab],
            send_sem=pass_send.at[step], recv_sem=pass_slab_recv.at[slab],
            device_id=mesh_at(to, tile),
        )
        copy.start()
        drains.append(copy.wait_send)
    by_slab[slab] = out_rows[slab]
    for step in range(1, slabs):
        origin = other_slab(step)
        pltpu.make_async_remote_copy(
            src_ref=out_rows.at[origin], dst_ref=by_slab.at[origin],
            send_sem=pass_send.at[step], recv_sem=pass_slab_recv.at[origin],
            device_id=mesh_at(origin, tile),
        ).wait_recv()
    for s in range(slabs):
        turned[pl.ds(s, tiles, stride=slabs), :] = by_slab[s]
    pl.semaphore_wait(row_in, lines - 1)
    for step in sorted(range(1, tiles), key=far):
        to = other_tile(step)
        copy = pltpu.make_async_remote_copy(
            src_ref=turned.at[pl.ds(to * slabs, slabs)], dst_ref=by_tile.at[pl.ds(tile * slabs, slabs)],
            send_sem=pass_send.at[slabs + step], recv_sem=pass_tile_recv.at[tile],
            device_id=mesh_at(slab, to),
        )
        copy.start()
        drains.append(copy.wait_send)
    by_tile[pl.ds(tile * slabs, slabs), :] = turned[pl.ds(tile * slabs, slabs), :]
    for step in range(1, tiles):
        origin = other_tile(step)
        pltpu.make_async_remote_copy(
            src_ref=turned.at[pl.ds(origin * slabs, slabs)], dst_ref=by_tile.at[pl.ds(origin * slabs, slabs)],
            send_sem=pass_send.at[slabs + step], recv_sem=pass_tile_recv.at[origin],
            device_id=mesh_at(slab, origin),
        ).wait_recv()

    lanes_first = by_tile[...].T
    owned = jnp.concatenate([lanes_first[32 * k : 32 * k + 32] for k in range(CAP)], axis=1)
    total = owned.shape[1]

    def spread_weights(cells, base, first, shift=0):
        offset = lax.broadcasted_iota(jnp.int32, (cells, total), 0).astype(F32) - (owned[base : base + 1] + float(shift))
        result = jnp.zeros((cells, total), F32)
        for step in range(4):
            result = jnp.where(offset == float(step), owned[first + step : first + step + 1], result)
        return result

    weight_z = spread_weights(8, 15, 0)
    weight_x = spread_weights(16, 16, 4, 2)
    weight_y = spread_weights(NY, 17, 8)
    plane = jnp.concatenate([weight_z[z : z + 1] * weight_x for z in range(CZ + 3)], axis=0)
    y_high, y_low = split(weight_y)
    y_reading = jnp.concatenate([y_high, y_high, y_low], axis=0)
    y_spreading = jnp.concatenate([y_high, y_high, y_low], axis=1)
    rows = (CZ + 3) * 16

    def spread(values):
        high, low = split(jnp.concatenate([plane * values[c] for c in range(3)], axis=0))
        result = lax.dot_general(
            jnp.concatenate([high, low, high], axis=1), y_spreading, NT, preferred_element_type=F32
        )
        return [
            jnp.concatenate(
                [result[c * rows + z * 16 : c * rows + z * 16 + 16] for c in range(3)], axis=1
            )
            for z in range(CZ + 3)
        ]

    def exists(s, t):
        inside = None
        if s:
            inside = (slab < slabs - s) if s > 0 else (slab >= -s)
        if t:
            along = (tile < tiles - t) if t > 0 else (tile >= -t)
            inside = along if inside is None else jnp.logical_and(inside, along)
        return inside

    def wide_copy(turn, number):
        entry = ROUNDS[turn][number]
        (s, t), (z, zs), (x, xs) = entry
        _, row, _ = landing(entry)
        return pltpu.make_async_remote_copy(
            src_ref=partial.at[turn, pl.ds(z, zs), pl.ds(x + 2, xs)],
            dst_ref=landed[turn][number].at[pl.ds(0, zs), pl.ds(row, xs)],
            send_sem=wide_send.at[turn, number], recv_sem=wide_recv.at[turn, number],
            device_id=mesh_at(wrapped(slab + s % slabs, slabs), wrapped(tile + t % tiles, tiles)),
        )

    def send_wide(turn):
        for number, entry in enumerate(ROUNDS[turn]):
            start_to(*entry[0], wide_copy(turn, number))

    def start_to(s, t, copy):
        @pl.when(exists(s, t))
        def _():
            copy.start()

        def drain():
            @pl.when(exists(s, t))
            def _():
                copy.wait_send()

        drains.append(drain)

    def wait_wide(turn):
        for number, entry in enumerate(ROUNDS[turn]):

            @pl.when(exists(-entry[0][0], -entry[0][1]))
            def _():
                wide_copy(turn, number).wait_recv()

    def added_up(turn, z):
        halves = [None, None]

        def add(half, value):
            halves[half] = value if halves[half] is None else halves[half] + value

        for number, entry in enumerate(ROUNDS[turn]):
            first, _, half = landing(entry)
            if first <= z < first + entry[1][1]:
                add(half, landed[turn][number][z - first])
        if z >= 2:
            add(0, partial[turn, z - 2, 0:8])
            add(1, partial[turn, z - 2, 8:16])
        return jnp.concatenate(halves, axis=0)

    def in_grid(value, z):
        keep = high_x if z < CZ else high_x & has_high_z
        return jnp.where(keep, value, 0.0)

    def read_samples(turn):
        values = jnp.concatenate(
            [
                field[turn, 2 : CZ + 5, :, c * NY : (c + 1) * NY].reshape(rows, NY)
                for c in range(3)
            ],
            axis=0,
        )
        high, low = split(values)
        seen = lax.dot_general(
            jnp.concatenate([high, low, high], axis=1), y_reading, NN, preferred_element_type=F32
        )
        return [
            jnp.sum(seen[c * rows : (c + 1) * rows] * plane, axis=0, keepdims=True) for c in range(3)
        ]

    lane = lax.broadcasted_iota(jnp.int32, (16, NY), 1)
    place = lax.broadcasted_iota(jnp.int32, (16, NY), 0)
    has_low_z, has_high_z = slab > 0, slab < slabs - 1
    own_x = (place >= 2) & (place < CX + 2)
    inside_x = own_x | ((place == CX + 2) & (tile < tiles - 1)) | ((place == 1) & (tile > 0))
    high_x = jnp.concatenate([(place < CX + 2) | (tile < tiles - 1)] * 3, axis=1)
    own_wide = jnp.concatenate([own_x] * 3, axis=1)

    def after_y(value):
        return jnp.where(lane == NY - 1, 0.0, pltpu.roll(value, NY - 1, 1))

    def before_y(value):
        return jnp.where(lane == 0, 0.0, pltpu.roll(value, 1, 1))

    def after_x(value):
        return pltpu.roll(value, 15, 0)

    def before_x(value):
        return pltpu.roll(value, 1, 0)

    def around(below, middle, above):
        total = (above + below) + (after_x(middle) + before_x(middle))
        return total + (after_y(middle) + before_y(middle)) - 6.0 * middle

    def cell(turn, c, z):
        return field[turn, z + 2, :, c * NY : (c + 1) * NY]

    def inside(value, z):
        keep = inside_x
        if z < 0:
            keep = keep & has_low_z
        if z >= CZ:
            keep = keep & has_high_z
        return jnp.where(keep, value, 0.0)

    def smooth(turn, layers):
        for c in range(3):
            for z in layers:
                value = around(cell(turn, c, z - 1), cell(turn, c, z), cell(turn, c, z + 1))
                bent[turn, c, z + 1] = inside(value, z)
        for z in layers:
            if z == CZ:
                continue
            along_z = cell(turn, 0, z + 1) - cell(turn, 0, z)
            along_x = after_x(cell(turn, 1, z)) - cell(turn, 1, z)
            along_y = after_y(cell(turn, 2, z)) - cell(turn, 2, z)
            source[turn, z + 1] = inside(along_z + along_x + along_y, z)

    div_weight = div_ref[0]
    bend_weight = bend_ref[0]

    def penalties(turn, c, z):
        here = source[turn, z + 1]
        if c == 0:
            pushed = source[turn, z] - here
        elif c == 1:
            pushed = before_x(here) - here
        else:
            pushed = before_y(here) - here
        again = around(bent[turn, c, z], bent[turn, c, z + 1], bent[turn, c, z + 2])
        return jnp.where(own_x, div_weight * pushed + bend_weight * again, 0.0)

    def all_penalties(turn):
        return [
            jnp.concatenate([penalties(turn, c, z) for c in range(3)], axis=1) for z in range(CZ)
        ]

    def one(values, keep=None):
        value = functools.reduce(jnp.add, values)
        if keep is not None:
            value = jnp.where(keep, value, 0.0)
        return jnp.sum(jnp.sum(value, axis=0, keepdims=True), axis=1, keepdims=True)

    row_lane = lax.broadcasted_iota(jnp.int32, (1, LANES), 1)

    me = slab * tiles + tile

    sizes = (slabs // 2, 2, lines, across)
    here = (lax.div(slab, 2), lax.rem(slab, 2), line, column)

    def opposite(step):
        return tuple(-k % size for k, size in zip(step, sizes))

    def distance(step):
        return sum(min(k, size - k) for k, size in zip(step[:1] + step[2:], sizes[:1] + sizes[2:])) + 0.1 * step[1]

    every = list(itertools.product(*(range(size) for size in sizes)))[1:]
    paired = sorted([step for step in every if step < opposite(step)], key=lambda step: -distance(step))
    alone = [step for step in every if step == opposite(step)]

    def send_rows(steps, turn):
        def at(axis, k):
            forward = wrapped(here[axis] + k, sizes[axis]) if k else here[axis]
            k = -k % sizes[axis]
            backward = wrapped(here[axis] + k, sizes[axis]) if k else here[axis]
            return forward if turn is None else jnp.where(turn == 0, forward, backward)

        z, core, y, x = ([at(axis, k) for k in range(sizes[axis])] for axis in range(4))
        to_slab = {(i, j): z[i] * 2 + core[j] for i in range(sizes[0]) for j in range(2)}
        to_tile = {(i, j): y[i] * across + x[j] for i in range(lines) for j in range(across)}
        for step in steps:
            pltpu.make_async_remote_copy(
                src_ref=sums.at[pl.ds(me, 1)], dst_ref=sums.at[pl.ds(me, 1)],
                send_sem=sum_sem.at[0], recv_sem=sum_sem.at[1],
                device_id=mesh_at(to_slab[step[:2]], to_tile[step[2:]]),
            ).start()

    def send_pairs(steps):
        def body(turn, carry):
            send_rows(steps, turn)
            return carry

        lax.fori_loop(0, 2, body, 0)

    def start_sum(values):
        row = jnp.zeros((1, LANES), F32)
        for number, value in enumerate(values):
            row = jnp.where(row_lane == number, value, row)
        sums[pl.ds(me, 1)] = row
        far_alone = [step for step in alone if distance(step) > 3]
        send_rows(far_alone, None)
        middle = len(paired) // 2
        send_pairs(paired[:middle])
        send_pairs(paired[middle:])
        send_rows([step for step in alone if step not in far_alone], None)

    def every_wait(number):
        others = sums.at[pl.ds(0, devices - 1)]
        pltpu.make_async_copy(others, others, sum_sem.at[number]).wait()

    def end_sum(number):
        every_wait(1)
        row = jnp.sum(sums[...], axis=0, keepdims=True)
        return [row[:, i : i + 1] for i in range(number)]

    for z, value in enumerate(spread([owned[12 + c : 13 + c] for c in range(3)])):
        partial[0, z] = value
    send_wide(0)
    wait_wide(0)
    for z in range(CZ + 5):
        field[0, z] = in_grid(added_up(0, z), z - 2)
    start = [field[0, z + 2] for z in range(CZ)]

    read_start = read_samples(0)
    smooth(0, range(-1, CZ + 1))

    def energy(readings, sources, bends):
        seen = one([v * v for v in readings])
        pushed = one([v * v for v in sources], own_x)
        again = one([v * v for v in bends], own_x)
        return seen + div_weight * pushed + bend_weight * again

    def own_source(turn):
        return [source[turn, z + 1] for z in range(CZ)]

    def own_bent(turn):
        return [bent[turn, c, z + 1] for c in range(3) for z in range(CZ)]

    held = all_penalties(0)
    fresh = spread(read_start)
    for z in range(CZ + 3):
        partial[1, z] = fresh[z] + held[z] if z < CZ else fresh[z]
    send_wide(1)
    square = one([v * v for v in start], own_wide)
    wait_wide(1)
    for z in range(CZ + 5):
        field[1, z] = in_grid(added_up(1, z), z - 2)
    image = [field[1, z + 2] for z in range(CZ)]

    read_image = read_samples(1)
    smooth(1, range(CZ))
    start_sum([
        square,
        one([v * y for v, y in zip(start, image)], own_wide),
        one([y * y for y in image], own_wide),
        energy(read_image, own_source(1), own_bent(1)),
    ])
    for z, value in enumerate(spread(read_image)):
        partial[2, z] = value
    send_wide(2)
    smooth(1, (-1, CZ))
    held = all_penalties(1)
    wait_wide(2)
    second = [added_up(2, z + 2) + held[z] for z in range(CZ)]
    finish()
    norm, curvature, image_square, image_energy = end_sum(4)

    step_size = norm / curvature
    left_square = step_size * step_size * image_square - norm
    ratio = left_square / norm
    left_image = curvature - step_size * image_square
    left_energy = left_image - step_size * (image_square - step_size * image_energy)
    bowed = left_energy + 2.0 * ratio * left_image + ratio * ratio * curvature
    step_next = left_square / bowed
    forward = step_size + step_next * (1.0 + ratio)
    backward = step_size * step_next
    for z in range(CZ):
        answer = forward * start[z] - backward * image[z]
        rest = (start[z] - forward * image[z]) + backward * second[z]
        for c in range(3):
            both_ref[0, c, z] = answer[2 : CX + 2, c * NY : (c + 1) * NY]
            both_ref[1, c, z] = rest[2 : CX + 2, c * NY : (c + 1) * NY]

    every_wait(0)


def local(slabs, tiles, owner, block_base, spline_weights, measured, div_weight, bend_weight):
    devices = slabs * tiles
    count = owner.shape[0]
    vmem = pl.BlockSpec(memory_space=pltpu.VMEM)
    dma = pltpu.SemaphoreType.DMA
    wide = 3 * NY
    out = pltpu.VMEM((2, 3, CZ, CX, NY), F32)
    both = pl.pallas_call(
        functools.partial(kernel, slabs, tiles),
        out_shape=out,
        in_specs=[pl.BlockSpec(memory_space=pltpu.HBM)] * 6,
        out_specs=vmem,
        scratch_shapes=[
            pltpu.VMEM((1, count), jnp.int32),
            pltpu.VMEM((3, count), jnp.int32),
            pltpu.VMEM((12, count), F32),
            pltpu.VMEM((3, count), F32),
            pltpu.SMEM((1,), F32),
            pltpu.SMEM((1,), F32),
            dma((6,)),
            pltpu.VMEM((32, count), F32),
            pltpu.VMEM((slabs, tiles, LANES), F32),
            pltpu.VMEM((slabs, tiles, LANES), F32),
            pltpu.VMEM((devices, LANES), F32),
            pltpu.VMEM((devices, LANES), F32),
            pltpu.VMEM((3, CZ + 3, 16, wide), F32),
            pltpu.VMEM((2, 9, 16, wide), F32),
            pltpu.VMEM((2, 3, CZ + 2, 16, NY), F32),
            pltpu.VMEM((2, CZ + 1, 16, NY), F32),
            dma((slabs + tiles,)),
            dma((slabs,)),
            dma((tiles,)),
            dma((3, len(WIDE))),
            dma((3, len(WIDE))),
            pltpu.VMEM((devices, LANES), F32),
            dma((2,)),
            pltpu.SemaphoreType.REGULAR,
        ]
        + [pltpu.VMEM((entry[1][1], 8, wide), F32) for entries in ROUNDS for entry in entries],
        compiler_params=pltpu.CompilerParams(collective_id=0, has_side_effects=True),
    )(owner.reshape(1, count), block_base, spline_weights, measured, div_weight, bend_weight)
    return both[0], both[1]


def solution(mesh):
    placed = (
        P(("slab", "tile"), None),
        P(None, ("slab", "tile")),
        P(None, ("slab", "tile")),
        P(None, ("slab", "tile")),
        P(),
        P(),
    )
    sizes = dict(zip(mesh.axis_names, mesh.devices.shape))
    return jax.shard_map(
        functools.partial(local, sizes["slab"], sizes["tile"]),
        mesh=mesh,
        in_specs=placed,
        out_specs=(P(None, "slab", "tile", None), P(None, "slab", "tile", None)),
        check_vma=False,
    )
```

```python
import functools
import itertools

import jax
import jax.numpy as jnp
from jax import lax
from jax.experimental import pallas as pl
from jax.experimental.pallas import tpu as pltpu
from jax.sharding import PartitionSpec as P

CZ = 4
CX = 8
NY = 128
CAP = 4
LANES = 128
F32 = jnp.float32
BF16 = jnp.bfloat16
NT = (((1,), (1,)), ((), ()))
NN = (((1,), (0,)), ((), ()))
WIDE = (
    ((2, 1), (6, 1), (8, 3)),
    ((1, 1), (2, 5), (6, 5)),
    ((-1, -1), (0, 3), (0, 3)),
    ((1, -1), (3, 4), (0, 3)),
    ((-1, 1), (0, 3), (7, 4)),
    ((0, 1), (0, 7), (6, 5)),
    ((0, -1), (0, 7), (0, 3)),
    ((2, 0), (6, 1), (0, 6)),
    ((2, 0), (6, 1), (6, 2)),
    ((1, 0), (2, 5), (0, 6)),
    ((1, 0), (2, 5), (6, 5)),
    ((-1, 0), (0, 3), (0, 6)),
    ((-1, 0), (0, 3), (6, 5)),
)
LAST = (
    ((1, 1), (4, 3), (8, 3)),
    ((0, 1), (0, 4), (8, 3)),
    ((1, 0), (4, 3), (0, 6)),
    ((1, 0), (4, 3), (6, 2)),
)
ROUNDS = (WIDE, WIDE, LAST)


def landing(entry):
    (s, t), (z, _), (x, _) = entry
    row = x - CX * t + 2
    return z - CZ * s + 2, row % 8, row // 8


def split(value):
    high = value.astype(BF16)
    return high, (value - high.astype(F32)).astype(BF16)


def wrapped(value, size):
    return jnp.where(value >= size, value - size, value)


def kernel(
    slabs, tiles, owner_in, base_in, spline_in, measured_in, div_in, bend_in,
    both_ref,
    owner_ref, base_ref, spline_ref, measured_ref, div_ref, bend_ref, load_sem,
    pay, out_rows, by_slab, turned, by_tile,
    partial, field, bent, source,
    pass_send, pass_slab_recv, pass_tile_recv, wide_send, wide_recv,
    sums, sum_sem, row_in,
    *landed,
):
    landed = (landed[: len(WIDE)], landed[len(WIDE) : 2 * len(WIDE)], landed[2 * len(WIDE) :])
    devices = slabs * tiles
    slab, tile = lax.axis_index("slab"), lax.axis_index("tile")
    count = owner_ref.shape[1]

    barrier = pltpu.get_barrier_semaphore()
    drains = []

    def finish():
        for drain in drains:
            drain()

    def mesh_at(s, t):
        return {"slab": s, "tile": t}

    def other_slab(step):
        return wrapped(slab + step, slabs)

    def other_tile(step):
        return wrapped(tile + step, tiles)

    across = 4 if tiles > 4 else 2
    column, line = lax.rem(tile, across), lax.div(tile, across)
    lines = tiles // across
    row_mates = [line * across + wrapped(column + step, across) for step in range(1, across)]
    column_mates = [wrapped(tile + step * across, tiles) for step in range(1, lines)]
    for step in sorted(range(1, slabs), key=lambda step: -min(step, slabs - step)):
        pl.semaphore_signal(barrier, inc=1, device_id=mesh_at(other_slab(step), tile))
    for mate in row_mates + column_mates:
        pl.semaphore_signal(barrier, inc=1, device_id=mesh_at(slab, mate))

    loads = [
        pltpu.make_async_copy(source, target, load_sem.at[number])
        for number, (source, target) in enumerate((
            (owner_in, owner_ref), (base_in, base_ref), (spline_in, spline_ref),
            (measured_in, measured_ref), (div_in, div_ref), (bend_in, bend_ref),
        ))
    ]
    for load in loads:
        load.start()

    def far(step):
        x, y = step % across, step // across
        return -(min(x, across - x) + min(y, lines - y))

    for buffers in landed:
        for buffer in buffers:
            buffer[...] = jnp.zeros_like(buffer)

    for load in loads:
        load.wait()

    pay[...] = jnp.zeros_like(pay)
    pay[0:12, :] = spline_ref[...]
    pay[12:15, :] = measured_ref[...]
    pay[15:18, :] = base_ref[...].astype(F32)
    owner = owner_ref[...]
    onehot = (lax.broadcasted_iota(jnp.int32, (devices, count), 0) == owner).astype(F32)
    onehot_b = onehot.astype(BF16)
    earlier = (
        lax.broadcasted_iota(jnp.int32, (count, count), 0)
        < lax.broadcasted_iota(jnp.int32, (count, count), 1)
    ).astype(BF16)
    before = lax.dot_general(onehot_b, earlier, NN, preferred_element_type=F32)
    rank = jnp.sum(onehot * before, axis=0, keepdims=True)
    payload = pay[...]
    slots = jnp.concatenate([jnp.where(rank == k, payload, 0.0) for k in range(CAP)], axis=0)
    high, low = split(slots)
    lowest = (slots - high.astype(F32) - low.astype(F32)).astype(BF16)
    rows = [lax.dot_general(onehot_b, part, NT, preferred_element_type=F32) for part in (high, low, lowest)]
    out_rows[...] = ((rows[0] + rows[1]) + rows[2]).reshape(slabs, tiles, LANES)

    pl.semaphore_wait(barrier, slabs - 1 + across - 1 + lines - 1)
    for mate in column_mates:
        pl.semaphore_signal(row_in, inc=1, device_id=mesh_at(slab, mate))

    for step in sorted(range(1, slabs), key=lambda step: -min(step, slabs - step)):
        to = other_slab(step)
        copy = pltpu.make_async_remote_copy(
            src_ref=out_rows.at[to], dst_ref=by_slab.at[slab],
            send_sem=pass_send.at[step], recv_sem=pass_slab_recv.at[slab],
            device_id=mesh_at(to, tile),
        )
        copy.start()
        drains.append(copy.wait_send)
    by_slab[slab] = out_rows[slab]
    for step in range(1, slabs):
        origin = other_slab(step)
        pltpu.make_async_remote_copy(
            src_ref=out_rows.at[origin], dst_ref=by_slab.at[origin],
            send_sem=pass_send.at[step], recv_sem=pass_slab_recv.at[origin],
            device_id=mesh_at(origin, tile),
        ).wait_recv()
    for s in range(slabs):
        turned[pl.ds(s, tiles, stride=slabs), :] = by_slab[s]
    pl.semaphore_wait(row_in, lines - 1)
    for step in sorted(range(1, tiles), key=far):
        to = wrapped(line + step // across, lines) * across + wrapped(column + step % across, across)
        copy = pltpu.make_async_remote_copy(
            src_ref=turned.at[pl.ds(to * slabs, slabs)], dst_ref=by_tile.at[pl.ds(tile * slabs, slabs)],
            send_sem=pass_send.at[slabs + step], recv_sem=pass_tile_recv.at[tile],
            device_id=mesh_at(slab, to),
        )
        copy.start()
        drains.append(copy.wait_send)
    by_tile[pl.ds(tile * slabs, slabs), :] = turned[pl.ds(tile * slabs, slabs), :]
    for step in range(1, tiles):
        origin = other_tile(step)
        pltpu.make_async_remote_copy(
            src_ref=turned.at[pl.ds(origin * slabs, slabs)], dst_ref=by_tile.at[pl.ds(origin * slabs, slabs)],
            send_sem=pass_send.at[slabs + step], recv_sem=pass_tile_recv.at[origin],
            device_id=mesh_at(slab, origin),
        ).wait_recv()

    lanes_first = by_tile[...].T
    owned = jnp.concatenate([lanes_first[32 * k : 32 * k + 32] for k in range(CAP)], axis=1)
    total = owned.shape[1]

    def spread_weights(cells, base, first, shift=0):
        offset = lax.broadcasted_iota(jnp.int32, (cells, total), 0).astype(F32) - (owned[base : base + 1] + float(shift))
        result = jnp.zeros((cells, total), F32)
        for step in range(4):
            result = jnp.where(offset == float(step), owned[first + step : first + step + 1], result)
        return result

    weight_z = spread_weights(8, 15, 0)
    weight_x = spread_weights(16, 16, 4, 2)
    weight_y = spread_weights(NY, 17, 8)
    plane = jnp.concatenate([weight_z[z : z + 1] * weight_x for z in range(CZ + 3)], axis=0)
    y_high, y_low = split(weight_y)
    y_reading = jnp.concatenate([y_high, y_high, y_low], axis=0)
    y_spreading = jnp.concatenate([y_high, y_high, y_low], axis=1)
    rows = (CZ + 3) * 16

    def spread(values):
        high, low = split(jnp.concatenate([plane * values[c] for c in range(3)], axis=0))
        result = lax.dot_general(
            jnp.concatenate([high, low, high], axis=1), y_spreading, NT, preferred_element_type=F32
        )
        return [
            jnp.concatenate(
                [result[c * rows + z * 16 : c * rows + z * 16 + 16] for c in range(3)], axis=1
            )
            for z in range(CZ + 3)
        ]

    def exists(s, t):
        inside = None
        if s:
            inside = (slab < slabs - s) if s > 0 else (slab >= -s)
        if t:
            along = (tile < tiles - t) if t > 0 else (tile >= -t)
            inside = along if inside is None else jnp.logical_and(inside, along)
        return inside

    def wide_copy(turn, number):
        entry = ROUNDS[turn][number]
        (s, t), (z, zs), (x, xs) = entry
        _, row, _ = landing(entry)
        return pltpu.make_async_remote_copy(
            src_ref=partial.at[turn, pl.ds(z, zs), pl.ds(x + 2, xs)],
            dst_ref=landed[turn][number].at[pl.ds(0, zs), pl.ds(row, xs)],
            send_sem=wide_send.at[turn, number], recv_sem=wide_recv.at[turn, number],
            device_id=mesh_at(wrapped(slab + s % slabs, slabs), wrapped(tile + t % tiles, tiles)),
        )

    def send_wide(turn):
        for number, entry in enumerate(ROUNDS[turn]):
            start_to(*entry[0], wide_copy(turn, number))

    def start_to(s, t, copy):
        @pl.when(exists(s, t))
        def _():
            copy.start()

        def drain():
            @pl.when(exists(s, t))
            def _():
                copy.wait_send()

        drains.append(drain)

    def wait_wide(turn):
        for number, entry in enumerate(ROUNDS[turn]):

            @pl.when(exists(-entry[0][0], -entry[0][1]))
            def _():
                wide_copy(turn, number).wait_recv()

    def added_up(turn, z):
        halves = [None, None]

        def add(half, value):
            halves[half] = value if halves[half] is None else halves[half] + value

        for number, entry in enumerate(ROUNDS[turn]):
            first, _, half = landing(entry)
            if first <= z < first + entry[1][1]:
                add(half, landed[turn][number][z - first])
        if z >= 2:
            add(0, partial[turn, z - 2, 0:8])
            add(1, partial[turn, z - 2, 8:16])
        return jnp.concatenate(halves, axis=0)

    def in_grid(value, z):
        keep = high_x if z < CZ else high_x & has_high_z
        return jnp.where(keep, value, 0.0)

    def read_samples(turn):
        values = jnp.concatenate(
            [
                field[turn, 2 : CZ + 5, :, c * NY : (c + 1) * NY].reshape(rows, NY)
                for c in range(3)
            ],
            axis=0,
        )
        high, low = split(values)
        seen = lax.dot_general(
            jnp.concatenate([high, low, high], axis=1), y_reading, NN, preferred_element_type=F32
        )
        return [
            jnp.sum(seen[c * rows : (c + 1) * rows] * plane, axis=0, keepdims=True) for c in range(3)
        ]

    lane = lax.broadcasted_iota(jnp.int32, (16, NY), 1)
    place = lax.broadcasted_iota(jnp.int32, (16, NY), 0)
    has_low_z, has_high_z = slab > 0, slab < slabs - 1
    own_x = (place >= 2) & (place < CX + 2)
    inside_x = own_x | ((place == CX + 2) & (tile < tiles - 1)) | ((place == 1) & (tile > 0))
    high_x = jnp.concatenate([(place < CX + 2) | (tile < tiles - 1)] * 3, axis=1)
    own_wide = jnp.concatenate([own_x] * 3, axis=1)

    def after_y(value):
        return jnp.where(lane == NY - 1, 0.0, pltpu.roll(value, NY - 1, 1))

    def before_y(value):
        return jnp.where(lane == 0, 0.0, pltpu.roll(value, 1, 1))

    def after_x(value):
        return pltpu.roll(value, 15, 0)

    def before_x(value):
        return pltpu.roll(value, 1, 0)

    def around(below, middle, above):
        total = (above + below) + (after_x(middle) + before_x(middle))
        return total + (after_y(middle) + before_y(middle)) - 6.0 * middle

    def cell(turn, c, z):
        return field[turn, z + 2, :, c * NY : (c + 1) * NY]

    def inside(value, z):
        keep = inside_x
        if z < 0:
            keep = keep & has_low_z
        if z >= CZ:
            keep = keep & has_high_z
        return jnp.where(keep, value, 0.0)

    def smooth(turn, layers):
        for c in range(3):
            for z in layers:
                value = around(cell(turn, c, z - 1), cell(turn, c, z), cell(turn, c, z + 1))
                bent[turn, c, z + 1] = inside(value, z)
        for z in layers:
            if z == CZ:
                continue
            along_z = cell(turn, 0, z + 1) - cell(turn, 0, z)
            along_x = after_x(cell(turn, 1, z)) - cell(turn, 1, z)
            along_y = after_y(cell(turn, 2, z)) - cell(turn, 2, z)
            source[turn, z + 1] = inside(along_z + along_x + along_y, z)

    div_weight = div_ref[0]
    bend_weight = bend_ref[0]

    def penalties(turn, c, z):
        here = source[turn, z + 1]
        if c == 0:
            pushed = source[turn, z] - here
        elif c == 1:
            pushed = before_x(here) - here
        else:
            pushed = before_y(here) - here
        again = around(bent[turn, c, z], bent[turn, c, z + 1], bent[turn, c, z + 2])
        return jnp.where(own_x, div_weight * pushed + bend_weight * again, 0.0)

    def all_penalties(turn):
        return [
            jnp.concatenate([penalties(turn, c, z) for c in range(3)], axis=1) for z in range(CZ)
        ]

    def one(values, keep=None):
        value = functools.reduce(jnp.add, values)
        if keep is not None:
            value = jnp.where(keep, value, 0.0)
        return jnp.sum(jnp.sum(value, axis=0, keepdims=True), axis=1, keepdims=True)

    row_lane = lax.broadcasted_iota(jnp.int32, (1, LANES), 1)

    me = slab * tiles + tile

    sizes = (slabs // 2, 2, lines, across)
    here = (lax.div(slab, 2), lax.rem(slab, 2), line, column)

    def opposite(step):
        return tuple(-k % size for k, size in zip(step, sizes))

    def distance(step):
        return sum(min(k, size - k) for k, size in zip(step[:1] + step[2:], sizes[:1] + sizes[2:])) + 0.1 * step[1]

    every = list(itertools.product(*(range(size) for size in sizes)))[1:]
    paired = sorted([step for step in every if step < opposite(step)], key=lambda step: -distance(step))
    alone = [step for step in every if step == opposite(step)]

    def send_rows(steps, turn):
        def at(axis, k):
            forward = wrapped(here[axis] + k, sizes[axis]) if k else here[axis]
            k = -k % sizes[axis]
            backward = wrapped(here[axis] + k, sizes[axis]) if k else here[axis]
            return forward if turn is None else jnp.where(turn == 0, forward, backward)

        z, core, y, x = ([at(axis, k) for k in range(sizes[axis])] for axis in range(4))
        to_slab = {(i, j): z[i] * 2 + core[j] for i in range(sizes[0]) for j in range(2)}
        to_tile = {(i, j): y[i] * across + x[j] for i in range(lines) for j in range(across)}
        for step in steps:
            pltpu.make_async_remote_copy(
                src_ref=sums.at[pl.ds(me, 1)], dst_ref=sums.at[pl.ds(me, 1)],
                send_sem=sum_sem.at[0], recv_sem=sum_sem.at[1],
                device_id=mesh_at(to_slab[step[:2]], to_tile[step[2:]]),
            ).start()

    def send_pairs(steps):
        def body(turn, carry):
            send_rows(steps, turn)
            return carry

        lax.fori_loop(0, 2, body, 0)

    def start_sum(values):
        row = jnp.zeros((1, LANES), F32)
        for number, value in enumerate(values):
            row = jnp.where(row_lane == number, value, row)
        sums[pl.ds(me, 1)] = row
        far_alone = [step for step in alone if distance(step) > 3]
        send_rows(far_alone, None)
        middle = len(paired) // 2
        send_pairs(paired[:middle])
        send_pairs(paired[middle:])
        send_rows([step for step in alone if step not in far_alone], None)

    def every_wait(number):
        others = sums.at[pl.ds(0, devices - 1)]
        pltpu.make_async_copy(others, others, sum_sem.at[number]).wait()

    def end_sum(number):
        every_wait(1)
        row = jnp.sum(sums[...], axis=0, keepdims=True)
        return [row[:, i : i + 1] for i in range(number)]

    for z, value in enumerate(spread([owned[12 + c : 13 + c] for c in range(3)])):
        partial[0, z] = value
    send_wide(0)
    wait_wide(0)
    for z in range(CZ + 5):
        field[0, z] = in_grid(added_up(0, z), z - 2)
    start = [field[0, z + 2] for z in range(CZ)]

    read_start = read_samples(0)
    smooth(0, range(-1, CZ + 1))

    def energy(readings, sources, bends):
        seen = one([v * v for v in readings])
        pushed = one([v * v for v in sources], own_x)
        again = one([v * v for v in bends], own_x)
        return seen + div_weight * pushed + bend_weight * again

    def own_source(turn):
        return [source[turn, z + 1] for z in range(CZ)]

    def own_bent(turn):
        return [bent[turn, c, z + 1] for c in range(3) for z in range(CZ)]

    held = all_penalties(0)
    fresh = spread(read_start)
    for z in range(CZ + 3):
        partial[1, z] = fresh[z] + held[z] if z < CZ else fresh[z]
    send_wide(1)
    square = one([v * v for v in start], own_wide)
    wait_wide(1)
    for z in range(CZ + 5):
        field[1, z] = in_grid(added_up(1, z), z - 2)
    image = [field[1, z + 2] for z in range(CZ)]

    read_image = read_samples(1)
    smooth(1, range(CZ))
    start_sum([
        square,
        one([v * y for v, y in zip(start, image)], own_wide),
        one([y * y for y in image], own_wide),
        energy(read_image, own_source(1), own_bent(1)),
    ])
    for z, value in enumerate(spread(read_image)):
        partial[2, z] = value
    send_wide(2)
    smooth(1, (-1, CZ))
    held = all_penalties(1)
    wait_wide(2)
    second = [added_up(2, z + 2) + held[z] for z in range(CZ)]
    finish()
    norm, curvature, image_square, image_energy = end_sum(4)

    step_size = norm / curvature
    left_square = step_size * step_size * image_square - norm
    ratio = left_square / norm
    left_image = curvature - step_size * image_square
    left_energy = left_image - step_size * (image_square - step_size * image_energy)
    bowed = left_energy + 2.0 * ratio * left_image + ratio * ratio * curvature
    step_next = left_square / bowed
    forward = step_size + step_next * (1.0 + ratio)
    backward = step_size * step_next
    for z in range(CZ):
        answer = forward * start[z] - backward * image[z]
        rest = (start[z] - forward * image[z]) + backward * second[z]
        for c in range(3):
            both_ref[0, c, z] = answer[2 : CX + 2, c * NY : (c + 1) * NY]
            both_ref[1, c, z] = rest[2 : CX + 2, c * NY : (c + 1) * NY]

    every_wait(0)


def local(slabs, tiles, owner, block_base, spline_weights, measured, div_weight, bend_weight):
    devices = slabs * tiles
    count = owner.shape[0]
    vmem = pl.BlockSpec(memory_space=pltpu.VMEM)
    dma = pltpu.SemaphoreType.DMA
    wide = 3 * NY
    out = pltpu.VMEM((2, 3, CZ, CX, NY), F32)
    both = pl.pallas_call(
        functools.partial(kernel, slabs, tiles),
        out_shape=out,
        in_specs=[pl.BlockSpec(memory_space=pltpu.HBM)] * 6,
        out_specs=vmem,
        scratch_shapes=[
            pltpu.VMEM((1, count), jnp.int32),
            pltpu.VMEM((3, count), jnp.int32),
            pltpu.VMEM((12, count), F32),
            pltpu.VMEM((3, count), F32),
            pltpu.SMEM((1,), F32),
            pltpu.SMEM((1,), F32),
            dma((6,)),
            pltpu.VMEM((32, count), F32),
            pltpu.VMEM((slabs, tiles, LANES), F32),
            pltpu.VMEM((slabs, tiles, LANES), F32),
            pltpu.VMEM((devices, LANES), F32),
            pltpu.VMEM((devices, LANES), F32),
            pltpu.VMEM((3, CZ + 3, 16, wide), F32),
            pltpu.VMEM((2, 9, 16, wide), F32),
            pltpu.VMEM((2, 3, CZ + 2, 16, NY), F32),
            pltpu.VMEM((2, CZ + 1, 16, NY), F32),
            dma((slabs + tiles,)),
            dma((slabs,)),
            dma((tiles,)),
            dma((3, len(WIDE))),
            dma((3, len(WIDE))),
            pltpu.VMEM((devices, LANES), F32),
            dma((2,)),
            pltpu.SemaphoreType.REGULAR,
        ]
        + [pltpu.VMEM((entry[1][1], 8, wide), F32) for entries in ROUNDS for entry in entries],
        compiler_params=pltpu.CompilerParams(collective_id=0, has_side_effects=True),
    )(owner.reshape(1, count), block_base, spline_weights, measured, div_weight, bend_weight)
    return both[0], both[1]


def solution(mesh):
    placed = (
        P(("slab", "tile"), None),
        P(None, ("slab", "tile")),
        P(None, ("slab", "tile")),
        P(None, ("slab", "tile")),
        P(),
        P(),
    )
    sizes = dict(zip(mesh.axis_names, mesh.devices.shape))
    return jax.shard_map(
        functools.partial(local, sizes["slab"], sizes["tile"]),
        mesh=mesh,
        in_specs=placed,
        out_specs=(P(None, "slab", "tile", None), P(None, "slab", "tile", None)),
        check_vma=False,
    )
```
